32 devices in a mesh: seq: 4 (over z), batch: 8 (over y, x, core).
Axes of the slice: x: 2, y: 2, z: 4, core: 2. Of those that a mesh axis runs over, the one named last changes fastest.
Arguments:
- queries: bfloat16 [8, 1024, 1024], P('batch', 'seq'), may hold values from -80 to 80
- keys: bfloat16 [8, 1024, 1024], P('batch', 'seq'), may hold values from -8 to 8
- values: bfloat16 [8, 1024, 1024], P('batch', 'seq'), may hold values from -6 to 6
- residual: bfloat16 [8, 1024, 1024], P('batch', 'seq'), may hold values from -2 to 2
- out_weight: bfloat16 [1024, 1024], replicated, may hold values from -0.1875 to 0.1875
- norm_gain: float32 [1024], replicated, may hold values from 0.1 to 1.9
- source_queue: bfloat16 [4096, 1024], P('batch'), may hold values from -32 to 32
- span_lengths: int32 [8, 64], P('batch'), may hold values from 1 to 32, 1024 in all within a row
- positives: int32 [8, 64], P(None, 'seq'), may hold values from 0 to 4095
Outputs:
- anchors: bfloat16 [8, 64, 1024], P('batch', 'seq')
- losses: float32 [8, 64], P('batch', 'seq')
The draws below stay inside these ranges and needn't reach their ends.
All inputs are finite; a program needn't handle non-finite values.
Results may differ from the reference program's by a relative error of at most 0.0047.
Values may be sent and summed in bfloat16 or wider, within the bound.
A program may use at most 64 MiB of HBM per device.

```python
import math
import jax
import jax.numpy as jnp
import numpy as np
from jax import lax

D = 1024
HEADS = 16
HEAD_DIM = 64
WINDOW = 512
FUNC_DEV = 16
BINARIES = 8
LENGTH = 1024
FUNCS = 64
FN_MOST = 32
QUEUE = 4096
N_SEQ = 4


def draw_pair(key):
    pair_key = jax.random.fold_in(key, 11)
    key_query, key_key = jax.random.split(pair_key, 2)
    full_shape = (BINARIES, LENGTH, D)
    query_part = jnp.clip(jax.random.normal(key_query, full_shape, jnp.float32), -6.0, 6.0)
    key_part = jnp.clip(jax.random.normal(key_key, full_shape, jnp.float32), -6.0, 6.0)
    return (query_part, key_part)


def draw_queries(key, part):
    return draw_pair(key)[0].astype(jnp.bfloat16)


def draw_keys(key, part):
    return draw_pair(key)[1].astype(jnp.bfloat16)


def draw_source_queue(key, part):
    key_rows = jax.random.fold_in(jax.random.fold_in(key, 23), 0)
    key_entries = jax.random.fold_in(jax.random.fold_in(key, 23), 2)
    row_scale = jnp.exp(jax.random.uniform(key_rows, (QUEUE, 1), jnp.float32, math.log(0.05), math.log(0.5)))
    entries = jnp.clip(jax.random.normal(key_entries, (QUEUE, D), jnp.float32), -6.0, 6.0)
    return (entries * row_scale).astype(jnp.bfloat16)


def set_ends(values, key, smallest, largest):
    longest = values.shape.index(max(values.shape))
    spots = []
    for shift in (0, 1):
        where = [jax.random.randint(jax.random.fold_in(key, axis), (), 0, length) for axis, length in enumerate(values.shape)]
        where[longest] = (where[longest] + shift) % values.shape[longest]
        spots.append(tuple(where))
    return values.at[spots[0]].set(smallest).at[spots[1]].set(largest)


def steps_of(stream_key, extent, shards, least, high):
    factor_of, own = 1.0, jax.random.fold_in(stream_key, 6)
    for axis_at, blocks in shards:
        draws = jnp.exp(jax.random.uniform(jax.random.fold_in(own, axis_at), (blocks,), jnp.float32, least / len(shards), high / len(shards)))
        factor_of = factor_of * jnp.repeat(draws, extent[axis_at] // blocks).reshape([-1 if axis == axis_at else 1 for axis in range(len(extent))])
    return factor_of


def profile(number_of, total, limit, slope):
    portions = [(1 << 20) // math.isqrt(rank ** slope) + 1 for rank in range(2, number_of + 1)]
    surplus, holding = total - limit - (number_of - 1), [1] * (number_of - 1)
    while surplus > 0:
        free = [i for i in range(number_of - 1) if holding[i] < limit]
        whole, budget = sum([portions[i] for i in free]), surplus
        for i in free:
            more = min(limit - holding[i], max(1, budget * portions[i] // whole), surplus)
            holding[i] = holding[i] + more
            surplus = surplus - more
    return np.array([limit] + holding)


def uneven_parts(rng, amount, total, most, skew):
    if amount == 2:
        one = jax.random.randint(rng, (), max(1, total - most), min(most, total - 1) + 1)
        return jnp.stack([one, total - one])
    sizes = jnp.asarray(profile(amount, total, most, skew), jnp.int32)
    twos = (amount - 1) // 2
    giver, receiver = sizes[1:1 + 2 * twos:2], sizes[2:2 + 2 * twos:2]
    slack = jnp.minimum(giver - 1, most - receiver)
    moved = jax.random.randint(jax.random.fold_in(rng, 1), (twos,), 0, 1 << 20) % (slack + 1)
    sizes = sizes.at[1:1 + 2 * twos:2].set(giver - moved).at[2:2 + 2 * twos:2].set(receiver + moved)
    return sizes[jax.random.permutation(jax.random.fold_in(rng, 2), amount)]


def normal_values(stream_key, shape, width, most, cuts=(), kind=jnp.bfloat16):
    drawn = jax.random.normal(stream_key, shape, jnp.float32) * width
    if len(cuts) > 0:
        drawn = steps_of(stream_key, shape, cuts, -0.22, 0.18) * drawn
    return jnp.clip(drawn, min=-most, max=most).astype(kind)


def setup_inputs(seed: int = 0) -> dict:
    streams_of = jax.random.split(jax.random.key(seed), 10)
    queries = draw_queries(jax.random.fold_in(streams_of[9], 71), 0)
    keys = draw_keys(jax.random.fold_in(streams_of[9], 71), 0)
    values = normal_values(streams_of[2], (BINARIES, LENGTH, D), 1.0, 6.0, ((0, 8), (1, 4)))
    residual = normal_values(streams_of[3], (BINARIES, LENGTH, D), 0.25, 2.0, ((0, 8), (1, 4)))
    out_weight = normal_values(streams_of[4], (D, D), D ** -0.5, 0.1875)
    norm_gain = jnp.clip(1.0 + 0.18 * jax.random.normal(streams_of[5], (D,), jnp.float32), 0.1, 1.9)
    source_queue = draw_source_queue(jax.random.fold_in(streams_of[9], 71), 0)
    span_lengths = jax.vmap(lambda own: uneven_parts(own, FUNCS, LENGTH, FN_MOST, 2))(jax.random.split(streams_of[7], BINARIES)).reshape((BINARIES, FUNCS)).astype(jnp.int32)
    positives = set_ends(jax.random.randint(streams_of[8], (BINARIES, FUNCS), 0, QUEUE), jax.random.fold_in(streams_of[8], 1), 0, QUEUE - 1).astype(jnp.int32)
    return {"queries": queries, "keys": keys, "values": values, "residual": residual, "out_weight": out_weight, "norm_gain": norm_gain, "source_queue": source_queue, "span_lengths": span_lengths, "positives": positives}


def attend(queries, keys, values):
    block_rows = math.gcd(LENGTH, 512)
    padded_keys = jnp.pad(keys, ((WINDOW, 0), (0, 0)))
    padded_values = jnp.pad(values, ((WINDOW, 0), (0, 0)))

    def one_block(block_index):
        first_row = block_index * block_rows
        query_block = lax.dynamic_slice(queries, (first_row, jnp.int32(0)), (block_rows, D))
        key_block = lax.dynamic_slice(padded_keys, (first_row, jnp.int32(0)), (block_rows + WINDOW, D))
        value_block = lax.dynamic_slice(padded_values, (first_row, jnp.int32(0)), (block_rows + WINDOW, D))
        query_pos = first_row + jnp.arange(block_rows, dtype=jnp.int32)
        key_pos = first_row - WINDOW + jnp.arange(block_rows + WINDOW, dtype=jnp.int32)
        distance = query_pos[:, None] - key_pos[None, :]
        allowed = (distance >= 0) & (distance < WINDOW) & (key_pos[None, :] >= 0)
        query_heads = query_block.reshape(block_rows, HEADS, HEAD_DIM).astype(jnp.float32)
        key_heads = key_block.reshape(block_rows + WINDOW, HEADS, HEAD_DIM).astype(jnp.float32)
        value_heads = value_block.reshape(block_rows + WINDOW, HEADS, HEAD_DIM).astype(jnp.float32)
        scores = jnp.einsum('qhd,khd->hqk', query_heads, key_heads) / math.sqrt(HEAD_DIM)
        scores = jnp.where(allowed[None], scores, -jnp.inf)
        row_peak = lax.optimization_barrier(jnp.max(scores, axis=-1, keepdims=True))
        exp_scores = jnp.exp(scores - row_peak)
        weights = (exp_scores / lax.optimization_barrier(jnp.sum(exp_scores, axis=-1, keepdims=True))).astype(jnp.bfloat16)
        mixed = jnp.einsum('hqk,khd->qhd', weights.astype(jnp.float32), value_heads)
        return mixed.astype(jnp.bfloat16).reshape(block_rows, D)
    blocks = lax.map(one_block, jnp.arange(LENGTH // block_rows, dtype=jnp.int32))
    return blocks.reshape(LENGTH, D)

def reference(queries, keys, values, residual, out_weight, norm_gain, source_queue, span_lengths, positives):

    def per_binary(binary_items):
        query_rows, key_rows, value_rows, stream, lengths, wanted = binary_items
        attended = attend(query_rows, key_rows, value_rows)
        hidden = stream.astype(jnp.float32) + jnp.dot(attended, out_weight, preferred_element_type=jnp.float32)
        scale = lax.rsqrt(lax.optimization_barrier(jnp.mean(hidden * hidden, axis=-1, keepdims=True)) + 1e-05)
        normed = (hidden * scale * norm_gain.astype(jnp.float32)).astype(jnp.bfloat16)
        span_ends = jnp.cumsum(lengths).astype(jnp.int32)
        starts = span_ends - lengths
        row_ids = jnp.arange(FUNCS, dtype=jnp.int32)
        listed = (row_ids % FUNC_DEV * N_SEQ + row_ids // FUNC_DEV).astype(jnp.int32)
        row_starts = jnp.take(starts, listed)
        row_ends = jnp.take(span_ends, listed)
        token_pos = jnp.arange(LENGTH, dtype=jnp.int32)
        member = ((token_pos[None, :] >= row_starts[:, None]) & (token_pos[None, :] < row_ends[:, None])).astype(jnp.bfloat16)
        pooled = jnp.dot(member, normed, preferred_element_type=jnp.float32)
        anchor_rows = (pooled * lax.rsqrt(lax.optimization_barrier(jnp.sum(pooled * pooled, axis=-1, keepdims=True)) + 1e-06)).astype(jnp.bfloat16)
        logits = 20.0 * jnp.dot(anchor_rows, source_queue.T, preferred_element_type=jnp.float32)
        row_peak = lax.optimization_barrier(jnp.max(logits, axis=-1))
        log_total = row_peak + jnp.log(lax.optimization_barrier(jnp.sum(jnp.exp(logits - row_peak[:, None]), axis=-1)))
        positive = jnp.take_along_axis(logits, wanted[:, None].astype(jnp.int32), axis=1)[:, 0]
        return (anchor_rows, log_total - positive)
    anchors, losses = lax.map(per_binary, (queries, keys, values, residual, span_lengths, positives))
    return (anchors, losses)
```

```python
import functools
import math

import jax
import jax.numpy as jnp
from jax import lax
from jax.experimental import pallas as pl
from jax.experimental.pallas import tpu as pltpu
from jax.sharding import PartitionSpec as P

HEADS = 16
WINDOW = 512
MESH = pl.DeviceIdType.MESH
F32 = jnp.float32
BF16 = jnp.bfloat16
LOGIT_SCALE = 20.0
NEVER = -1e30
AHEAD = 3
LOOKAHEAD = 2
ROWS_T = (((1,), (1,)), ((), ()))


def attend(query_chunk, key_blocks, head_size):
    tok_rows, width = query_chunk.shape
    half = tok_rows // 2
    to_log2 = math.log2(math.e) / math.sqrt(head_size)
    heads = width // head_size
    lane = lax.broadcasted_iota(jnp.int32, (tok_rows, width), 1)
    query_less_key = lax.broadcasted_iota(jnp.int32, (half, half), 1) - lax.broadcasted_iota(
        jnp.int32, (half, half), 0
    )
    units = [(h, i) for h in range(heads) for i in range(2)]

    def spans(i):
        found = []
        for key_ref, value_t, apart in key_blocks:
            offsets = [apart * tok_rows + (i - j) * half for j in range(2)]
            seen = [j for j in range(2) if -half < offsets[j] < WINDOW + half - 1]
            found.append((key_ref, value_t, offsets, seen))
        return found

    def scores_of(h, i):
        own = (lane >= h * head_size) & (lane < (h + 1) * head_size)
        query_h = jnp.where(own, query_chunk, jnp.zeros_like(query_chunk))
        query_h = query_h[i * half : (i + 1) * half]
        return [
            lax.dot_general(
                key_ref[seen[0] * half : (seen[-1] + 1) * half, :],
                query_h,
                ROWS_T,
                preferred_element_type=F32,
            )
            for key_ref, _, _, seen in spans(i)
        ]

    def finish(h, i, scores):
        blocks = []
        for (_, _, offsets, seen), score in zip(spans(i), scores):
            parts = []
            for j in seen:
                part = score[(j - seen[0]) * half : (j - seen[0] + 1) * half]
                if offsets[j] < half - 1:
                    part = jnp.where(query_less_key >= -offsets[j], part, NEVER)
                if offsets[j] + half - 1 >= WINDOW:
                    part = jnp.where(query_less_key < WINDOW - offsets[j], part, NEVER)
                parts.append(part)
            blocks.append(parts)
        peak = functools.reduce(
            jnp.maximum,
            [jnp.max(part, axis=0, keepdims=True) for parts in blocks for part in parts],
        )
        blocks = [[jnp.exp2((part - peak) * to_log2) for part in parts] for parts in blocks]
        total = sum(jnp.sum(part, axis=0, keepdims=True) for parts in blocks for part in parts)
        mixed = sum(
            jnp.dot(
                value_t[
                    h * head_size : (h + 1) * head_size, seen[0] * half : (seen[-1] + 1) * half
                ],
                jnp.concatenate([part.astype(BF16) for part in parts], axis=0),
                preferred_element_type=F32,
            )
            for (_, value_t, _, seen), parts in zip(spans(i), blocks)
        )
        return mixed * (1.0 / total), peak * to_log2 + jnp.log2(total)

    pending, results = {}, {}
    for u in range(len(units) + LOOKAHEAD):
        if u < len(units):
            pending[u] = scores_of(*units[u])
        if u >= LOOKAHEAD:
            at = u - LOOKAHEAD
            results[units[at]] = finish(*units[at], pending.pop(at))
    mixed = jnp.concatenate(
        [jnp.concatenate([results[h, i][0] for i in range(2)], axis=1) for h in range(heads)],
        axis=0,
    )
    logs = jnp.concatenate(
        [jnp.concatenate([results[h, i][1] for i in range(2)], axis=1) for h in range(heads)],
        axis=0,
    )
    return mixed, logs


def merge(parts, heads, head_size):
    mixed = []
    for h in range(heads):
        logs = [log[h : h + 1] for _, log in parts]
        top = functools.reduce(jnp.maximum, logs)
        shares = [jnp.exp2(log - top) for log in logs]
        scale = 1.0 / sum(shares)
        rows = slice(h * head_size, (h + 1) * head_size)
        mixed.append(sum(mix[rows].astype(F32) * (s * scale) for (mix, _), s in zip(parts, shares)))
    return jnp.concatenate(mixed, axis=0).astype(BF16)


def block_kernel(
    n_seq,
    n_batch,
    head_size,
    gain_ref,
    lengths_ref,
    wanted_ref,
    queries_hbm,
    keys_hbm,
    values_hbm,
    residual_hbm,
    weight_hbm,
    queue_hbm,
    anchors_ref,
    losses_ref,
    q_own,
    k_own,
    v_own,
    v_t,
    q_near,
    q_far,
    k_first,
    v_t_first,
    mix_own,
    log_own,
    near_out,
    near_out_log,
    far_out,
    far_out_log,
    near_in,
    near_in_log,
    far_in,
    far_in_log,
    att_t,
    residual,
    weight,
    hidden,
    member,
    queue,
    parts,
    parts_in,
    logits,
    chunk_sem,
    load_sem,
    send_sem,
    recv_sem,
    part_send,
    part_recv,
    queue_send,
    queue_recv,
):
    chunks, tok_rows, chunk_cols = q_own.shape
    heads = chunk_cols // head_size
    own_rows, width = anchors_ref.shape
    funcs = own_rows * n_seq
    pieces, piece_rows = queue.shape[1:3]
    queue_rows = pieces * piece_rows
    seq = lax.axis_index("seq")
    batch = lax.axis_index("batch")

    def load(which, g):
        source = (queries_hbm, keys_hbm, values_hbm)[which]
        target = (q_own, k_own, v_own)[which]
        cols = pl.ds(pl.multiple_of(g * chunk_cols, chunk_cols), chunk_cols)
        return pltpu.make_async_copy(
            source.at[:, cols], target.at[g], chunk_sem.at[which, g]
        )

    def start_loads(g, carry):
        for which in range(3):
            load(which, g).start()
        return carry

    lax.fori_loop(0, chunks, start_loads, 0)
    queue_load = pltpu.make_async_copy(queue_hbm, queue.at[batch], load_sem.at[2])
    residual_load = pltpu.make_async_copy(residual_hbm, residual, load_sem.at[0])
    weight_load = pltpu.make_async_copy(weight_hbm, weight, load_sem.at[1])
    queue_load.start()
    residual_load.start()
    weight_load.start()

    core = lax.rem(batch, 2)
    row = lax.rem(batch // 2, 2)
    col = batch // 4
    n_col = n_batch // 4

    def shard_at(c, r, k):
        return (c * 2 + r) * 2 + k

    cols_away = [lax.rem(col + d, n_col) for d in range(1, n_col)]
    sibling = shard_at(col, row, 1 - core)
    across = shard_at(col, 1 - row, core)
    along = [shard_at(c, row, core) for c in cols_away]
    diagonal = [shard_at(c, 1 - row, core) for c in cols_away]
    queue_peers = [sibling, across] + along

    seq_peers = [lax.rem(seq + d, n_seq) for d in range(1, n_seq)]
    barrier = pltpu.get_barrier_semaphore()
    for peer in seq_peers:
        pl.semaphore_signal(barrier, inc=1, device_id={"seq": peer}, device_id_type=MESH)
    for peer in queue_peers:
        pl.semaphore_signal(barrier, inc=1, device_id={"batch": peer}, device_id_type=MESH)
    pl.semaphore_wait(barrier, n_seq - 1 + len(queue_peers))

    is_first = seq == 0
    is_second = seq == 1
    later = seq >= 2
    has_near = seq <= n_seq - 2

    def remote(kind, source, target, g, peer):
        return pltpu.make_async_remote_copy(
            src_ref=source.at[g],
            dst_ref=target.at[g],
            send_sem=send_sem.at[kind, g],
            recv_sem=recv_sem.at[kind, g],
            device_id={"seq": peer},
            device_id_type=MESH,
        )

    left, left_two = lax.rem(seq + n_seq - 1, n_seq), lax.rem(seq + n_seq - 2, n_seq)
    right, right_two = lax.rem(seq + 1, n_seq), lax.rem(seq + 2, n_seq)

    def ask_near(g):
        return remote(0, q_own, q_near, g, left)

    def ask_far(g):
        return remote(1, q_own, q_far, g, left_two)

    def give_near(g):
        return (
            remote(2, near_out_log, near_in_log, g, right),
            remote(3, near_out, near_in, g, right),
        )

    def give_far(g):
        return (
            remote(4, far_out_log, far_in_log, g, right_two),
            remote(5, far_out, far_in, g, right_two),
        )

    def give_keys(g):
        return remote(6, k_own, k_first, g, right)

    def give_values(g):
        return remote(7, v_t, v_t_first, g, right)

    def ask(g):
        load(0, g).wait()

        @pl.when(seq >= 3)
        def _():
            ask_far(g).start()

        @pl.when(later)
        def _():
            ask_near(g).start()

    def queue_copy(p, shard, k):
        return pltpu.make_async_remote_copy(
            src_ref=queue.at[shard, k],
            dst_ref=queue.at[shard, k],
            send_sem=queue_send.at[p, shard, k],
            recv_sem=queue_recv.at[shard, k],
            device_id={"batch": queue_peers[p]},
            device_id_type=MESH,
        )

    def spread_own(k, carry):
        for p in range(len(queue_peers)):
            queue_copy(p, batch, k).start()
        return carry

    def pass_on(k, act):
        act(queue_copy(0, across, k))
        for shard in along:
            act(queue_copy(0, shard, k))

        @pl.when(lax.rem(k, 2) == 0)
        def _():
            for p in range(len(along)):
                act(queue_copy(2 + p, across, k))

        @pl.when(lax.rem(k, 2) == 1)
        def _():
            for shard in along:
                act(queue_copy(1, shard, k))

    def forward(k):
        for shard in [across] + along:
            queue_copy(0, shard, k).wait_recv()
        pass_on(k, lambda copy: copy.start())

    ahead = min(AHEAD, chunks)
    for g in range(ahead):
        ask(g)
    queue_load.wait()
    lax.fori_loop(0, pieces, spread_own, 0)

    row_ids = lax.broadcasted_iota(jnp.int32, (funcs, funcs), 0)
    func_ids = lax.broadcasted_iota(jnp.int32, (funcs, funcs), 1)
    listed = lax.rem(row_ids, own_rows) * n_seq + row_ids // own_rows
    lengths = jnp.broadcast_to(lengths_ref[...].astype(F32), (funcs, funcs))
    begin_at = jnp.sum(jnp.where(func_ids < listed, lengths, 0.0), axis=1, keepdims=True)
    end_at = jnp.sum(jnp.where(func_ids <= listed, lengths, 0.0), axis=1, keepdims=True)
    pos = (
        seq * tok_rows + lax.broadcasted_iota(jnp.int32, (funcs, tok_rows), 1)
    ).astype(F32)
    member[...] = jnp.where((pos >= begin_at) & (pos < end_at), 1.0, 0.0).astype(BF16)

    def near_to(g, blocks):
        mixed, logs = attend(q_near[g], blocks, head_size)
        near_out_log[g] = logs
        near_out[g] = mixed.astype(BF16)
        for copy in give_near(g):
            copy.start()

    def far_to(g):
        ask_far(g).wait_recv()
        mixed, logs = attend(q_far[g], [(k_own.at[g], v_t.at[g], 2)], head_size)
        far_out_log[g] = logs
        far_out[g] = mixed.astype(BF16)
        for copy in give_far(g):
            copy.start()

    def step(g, carry):
        load(1, g).wait()
        load(2, g).wait()
        v_t[g] = v_own[g].T

        @pl.when(g + ahead < chunks)
        def _():
            ask(g + ahead)

        @pl.when(is_first)
        def _():
            @pl.when(g >= ahead)
            def _():
                give_keys(g - ahead).wait_send()
                give_values(g - ahead).wait_send()

            give_keys(g).start()
            give_values(g).start()
            mixed, _ = attend(q_own[g], [(k_own.at[g], v_t.at[g], 0)], head_size)
            att_t[g] = mixed.astype(BF16)

        @pl.when(is_second)
        def _():
            give_keys(g).wait_recv()
            give_values(g).wait_recv()
            ask_near(g).wait_recv()
            near_to(g, [(k_own.at[g], v_t.at[g], 1), (k_first.at[g], v_t_first.at[g], 2)])
            far_to(g)
            mixed, _ = attend(
                q_own[g],
                [(k_own.at[g], v_t.at[g], 0), (k_first.at[g], v_t_first.at[g], 1)],
                head_size,
            )
            att_t[g] = mixed.astype(BF16)

        @pl.when(later & has_near)
        def _():
            ask_near(g).wait_recv()
            near_to(g, [(k_own.at[g], v_t.at[g], 1)])

        if n_seq > 4:

            @pl.when(later & (seq <= n_seq - 3))
            def _():
                far_to(g)

        @pl.when(later)
        def _():
            mixed, logs = attend(q_own[g], [(k_own.at[g], v_t.at[g], 0)], head_size)
            mix_own[g] = mixed
            log_own[g] = logs

        @pl.when((g >= 1) & (g <= pieces))
        def _():
            forward(g - 1)

        return carry

    lax.fori_loop(0, chunks, step, 0)

    residual_load.wait()
    weight_load.wait()
    hidden[...] = residual[...].astype(F32)
    pair = 2

    def project(t, carry):
        for n in range(pair):
            g = t * pair + n

            @pl.when(seq == 2)
            def _():
                for copy in give_near(g):
                    copy.wait_recv()
                att_t[g] = merge(
                    [(mix_own[g], log_own[g]), (near_in[g], near_in_log[g])], heads, head_size
                )

            @pl.when(seq >= 3)
            def _():
                for copy in give_near(g) + give_far(g):
                    copy.wait_recv()
                att_t[g] = merge(
                    [
                        (mix_own[g], log_own[g]),
                        (near_in[g], near_in_log[g]),
                        (far_in[g], far_in_log[g]),
                    ],
                    heads,
                    head_size,
                )

        depth = pair * chunk_cols
        hidden[...] += lax.dot_general(
            att_t[pl.ds(t * pair, pair)].reshape(depth, tok_rows),
            weight[pl.ds(pl.multiple_of(t * depth, depth), depth), :],
            (((0,), (0,)), ((), ())),
            preferred_element_type=F32,
        )
        return carry

    lax.fori_loop(0, chunks // pair, project, 0)

    total = hidden[...]
    scale = lax.rsqrt(jnp.mean(total * total, axis=-1, keepdims=True) + 1e-05)
    normed = (total * scale * gain_ref[...]).astype(BF16)
    partial = jnp.dot(member[...], normed, preferred_element_type=F32)
    parts[...] = partial.reshape(n_seq, own_rows, width).astype(BF16)
    copies = []
    for d in range(1, n_seq):
        copy = pltpu.make_async_remote_copy(
            src_ref=parts.at[seq_peers[d - 1]],
            dst_ref=parts_in.at[d - 1],
            send_sem=part_send.at[d - 1],
            recv_sem=part_recv.at[d - 1],
            device_id={"seq": seq_peers[d - 1]},
            device_id_type=MESH,
        )
        copy.start()
        copies.append(copy)

    for k in range(min(chunks - 1, pieces), pieces):
        forward(k)

    def forward_diagonal(k, carry):
        for shard in diagonal:
            queue_copy(0, shard, k).wait_recv()
            queue_copy(0, shard, k).start()
        return carry

    lax.fori_loop(0, pieces, forward_diagonal, 0)

    pooled = parts[seq].astype(F32)
    for d in range(1, n_seq):
        copies[d - 1].wait_recv()
        pooled = pooled + parts_in[d - 1].astype(F32)
    anchors = (
        pooled * lax.rsqrt(jnp.sum(pooled * pooled, axis=-1, keepdims=True) + 1e-06)
    ).astype(BF16)
    anchors_ref[...] = anchors

    def logits_of(shard):
        logits[shard] = LOGIT_SCALE * lax.dot_general(
            anchors,
            queue[shard].reshape(queue_rows, width),
            ROWS_T,
            preferred_element_type=F32,
        )

    def await_shard(shard):
        def one(k, carry):
            queue_copy(0, shard, k).wait_recv()
            return carry

        lax.fori_loop(0, pieces, one, 0)

    for shard in [batch, across] + along + diagonal:
        logits_of(shard)
    beside = [shard_at(col, row, 1 - core), shard_at(col, 1 - row, 1 - core)]
    beside += [shard_at(c, r, 1 - core) for r in (row, 1 - row) for c in cols_away]
    for shard in beside:
        await_shard(shard)
        logits_of(shard)

    square = (own_rows, own_rows)
    on_diagonal = lax.broadcasted_iota(jnp.int32, square, 0) == lax.broadcasted_iota(
        jnp.int32, square, 1
    )
    wanted = jnp.broadcast_to(wanted_ref[pl.ds(batch, 1), :].astype(F32), square)
    wanted = jnp.sum(jnp.where(on_diagonal, wanted, 0.0), axis=1, keepdims=True)
    wanted = wanted.astype(jnp.int32)
    peak = functools.reduce(
        jnp.maximum, [jnp.max(logits[b], axis=1, keepdims=True) for b in range(n_batch)]
    )
    lane = lax.broadcasted_iota(jnp.int32, (own_rows, queue_rows), 1)
    sums, chosen = 0.0, 0.0
    for b in range(n_batch):
        sums = sums + jnp.exp(logits[b] - peak)
        chosen = chosen + jnp.where(lane + b * queue_rows == wanted, logits[b], 0.0)
    loss = (
        peak
        + jnp.log(jnp.sum(sums, axis=1, keepdims=True))
        - jnp.sum(chosen, axis=1, keepdims=True)
    )
    losses_ref[...] = jnp.sum(
        jnp.where(on_diagonal, jnp.broadcast_to(loss, square), 0.0), axis=0, keepdims=True
    )

    for copy in copies:
        copy.wait_send()

    def drain_queue(k, carry):
        for p in range(len(queue_peers)):
            queue_copy(p, batch, k).wait_send()
        pass_on(k, lambda copy: copy.wait_send())
        for shard in diagonal:
            queue_copy(0, shard, k).wait_send()
        return carry

    lax.fori_loop(0, pieces, drain_queue, 0)

    def drain(g, carry):
        @pl.when(is_first & (g >= chunks - ahead))
        def _():
            give_keys(g).wait_send()
            give_values(g).wait_send()

        @pl.when(later)
        def _():
            ask_near(g).wait_send()

        @pl.when(seq >= 3)
        def _():
            ask_far(g).wait_send()

        @pl.when((seq >= 1) & has_near)
        def _():
            for copy in give_near(g):
                copy.wait_send()

        @pl.when((seq >= 1) & (seq <= n_seq - 3))
        def _():
            for copy in give_far(g):
                copy.wait_send()

        return carry

    lax.fori_loop(0, chunks, drain, 0)


def body(
    queries, keys, values, residual, out_weight, norm_gain, source_queue, span_lengths, positives
):
    tok_rows, width = queries.shape[1:]
    head_size = width // HEADS
    n_seq = lax.axis_size("seq")
    n_batch = lax.axis_size("batch")
    own_rows = positives.shape[1]
    queue_rows = source_queue.shape[0]
    chunk_cols = 128
    chunks = width // chunk_cols
    pieces = max(2, 64 // n_batch)
    piece_rows = queue_rows // pieces
    assert (WINDOW - 1) // tok_rows + 1 == 2 and chunk_cols % head_size == 0
    assert n_seq >= 4 and n_batch % 4 == 0 and pieces % 2 == 0 and piece_rows % 16 == 0
    vmem = pl.BlockSpec(memory_space=pltpu.VMEM)
    hbm = pl.BlockSpec(memory_space=pl.ANY)
    rows_bf16 = pltpu.VMEM((chunks, tok_rows, chunk_cols), BF16)
    cols_bf16 = pltpu.VMEM((chunks, chunk_cols, tok_rows), BF16)
    cols_f32 = pltpu.VMEM((chunks, chunk_cols, tok_rows), F32)
    log_f32 = pltpu.VMEM((chunks, chunk_cols // head_size, tok_rows), F32)
    anchors, losses = pl.pallas_call(
        functools.partial(block_kernel, n_seq, n_batch, head_size),
        out_shape=(
            jax.ShapeDtypeStruct((own_rows, width), BF16),
            jax.ShapeDtypeStruct((1, own_rows), F32),
        ),
        in_specs=[vmem] * 3 + [hbm] * 6,
        out_specs=(vmem, vmem),
        scratch_shapes=[
            rows_bf16,
            rows_bf16,
            rows_bf16,
            cols_bf16,
            rows_bf16,
            rows_bf16,
            rows_bf16,
            cols_bf16,
            cols_f32,
            log_f32,
            cols_bf16,
            log_f32,
            cols_bf16,
            log_f32,
            cols_bf16,
            log_f32,
            cols_bf16,
            log_f32,
            cols_bf16,
            pltpu.VMEM((tok_rows, width), BF16),
            pltpu.VMEM(out_weight.shape, BF16),
            pltpu.VMEM((tok_rows, width), F32),
            pltpu.VMEM((own_rows * n_seq, tok_rows), BF16),
            pltpu.VMEM((n_batch, pieces, piece_rows, width), BF16),
            pltpu.VMEM((n_seq, own_rows, width), BF16),
            pltpu.VMEM((n_seq - 1, own_rows, width), BF16),
            pltpu.VMEM((n_batch, own_rows, queue_rows), F32),
            pltpu.SemaphoreType.DMA((3, chunks)),
            pltpu.SemaphoreType.DMA((3,)),
            pltpu.SemaphoreType.DMA((8, chunks)),
            pltpu.SemaphoreType.DMA((8, chunks)),
            pltpu.SemaphoreType.DMA((n_seq - 1,)),
            pltpu.SemaphoreType.DMA((n_seq - 1,)),
            pltpu.SemaphoreType.DMA((1 + n_batch // 4, n_batch, pieces)),
            pltpu.SemaphoreType.DMA((n_batch, pieces)),
        ],
        compiler_params=pltpu.CompilerParams(
            collective_id=0, has_side_effects=True, vmem_limit_bytes=67043328
        ),
        name="block",
    )(
        norm_gain.reshape(1, -1),
        span_lengths,
        positives,
        queries[0],
        keys[0],
        values[0],
        residual[0],
        out_weight,
        source_queue.reshape(pieces, piece_rows, width),
    )
    return (anchors[None], losses)


def solution(mesh):
    return jax.shard_map(
        body,
        mesh=mesh,
        in_specs=(
            P("batch", "seq", None),
            P("batch", "seq", None),
            P("batch", "seq", None),
            P("batch", "seq", None),
            P(),
            P(),
            P("batch", None),
            P("batch", None),
            P(None, "seq"),
        ),
        out_specs=(P("batch", "seq", None), P("batch", "seq")),
        check_vma=False,
    )
```

```python
import functools
import math

import jax
import jax.numpy as jnp
from jax import lax
from jax.experimental import pallas as pl
from jax.experimental.pallas import tpu as pltpu
from jax.sharding import PartitionSpec as P

HEADS = 16
WINDOW = 512
MESH = pl.DeviceIdType.MESH
F32 = jnp.float32
BF16 = jnp.bfloat16
LOGIT_SCALE = 20.0
NEVER = -1e30
LOOKAHEAD = 2
ROWS_T = (((1,), (1,)), ((), ()))


def attend(query_chunk, key_blocks, head_size):
    tok_rows, width = query_chunk.shape
    half = tok_rows // 2
    to_log2 = math.log2(math.e) / math.sqrt(head_size)
    heads = width // head_size
    lane = lax.broadcasted_iota(jnp.int32, (tok_rows, width), 1)
    query_less_key = lax.broadcasted_iota(jnp.int32, (half, half), 1) - lax.broadcasted_iota(
        jnp.int32, (half, half), 0
    )
    units = [(h, i) for h in range(heads) for i in range(2)]

    def spans(i):
        found = []
        for key_ref, value_t, apart in key_blocks:
            offsets = [apart * tok_rows + (i - j) * half for j in range(2)]
            seen = [j for j in range(2) if -half < offsets[j] < WINDOW + half - 1]
            found.append((key_ref, value_t, offsets, seen))
        return found

    def scores_of(h, i):
        own = (lane >= h * head_size) & (lane < (h + 1) * head_size)
        query_h = jnp.where(own, query_chunk, jnp.zeros_like(query_chunk))
        query_h = query_h[i * half : (i + 1) * half]
        return [
            lax.dot_general(
                key_ref[seen[0] * half : (seen[-1] + 1) * half, :],
                query_h,
                ROWS_T,
                preferred_element_type=F32,
            )
            for key_ref, _, _, seen in spans(i)
        ]

    def finish(h, i, scores):
        blocks = []
        for (_, _, offsets, seen), score in zip(spans(i), scores):
            parts = []
            for j in seen:
                part = score[(j - seen[0]) * half : (j - seen[0] + 1) * half]
                if offsets[j] < half - 1:
                    part = jnp.where(query_less_key >= -offsets[j], part, NEVER)
                if offsets[j] + half - 1 >= WINDOW:
                    part = jnp.where(query_less_key < WINDOW - offsets[j], part, NEVER)
                parts.append(part)
            blocks.append(parts)
        peak = functools.reduce(
            jnp.maximum,
            [jnp.max(part, axis=0, keepdims=True) for parts in blocks for part in parts],
        )
        blocks = [[jnp.exp2((part - peak) * to_log2) for part in parts] for parts in blocks]
        total = sum(jnp.sum(part, axis=0, keepdims=True) for parts in blocks for part in parts)
        mixed = sum(
            jnp.dot(
                value_t[
                    h * head_size : (h + 1) * head_size, seen[0] * half : (seen[-1] + 1) * half
                ],
                jnp.concatenate([part.astype(BF16) for part in parts], axis=0),
                preferred_element_type=F32,
            )
            for (_, value_t, _, seen), parts in zip(spans(i), blocks)
        )
        return mixed * (1.0 / total), peak * to_log2 + jnp.log2(total)

    pending, results = {}, {}
    for u in range(len(units) + LOOKAHEAD):
        if u < len(units):
            pending[u] = scores_of(*units[u])
        if u >= LOOKAHEAD:
            at = u - LOOKAHEAD
            results[units[at]] = finish(*units[at], pending.pop(at))
    mixed = jnp.concatenate(
        [jnp.concatenate([results[h, i][0] for i in range(2)], axis=1) for h in range(heads)],
        axis=0,
    )
    logs = jnp.concatenate(
        [jnp.concatenate([results[h, i][1] for i in range(2)], axis=1) for h in range(heads)],
        axis=0,
    )
    return mixed, logs


def merge(parts, heads, head_size):
    mixed = []
    for h in range(heads):
        logs = [log[h : h + 1] for _, log in parts]
        top = functools.reduce(jnp.maximum, logs)
        shares = [jnp.exp2(log - top) for log in logs]
        scale = 1.0 / sum(shares)
        rows = slice(h * head_size, (h + 1) * head_size)
        mixed.append(sum(mix[rows].astype(F32) * (s * scale) for (mix, _), s in zip(parts, shares)))
    return jnp.concatenate(mixed, axis=0).astype(BF16)


def block_kernel(
    n_seq,
    n_batch,
    head_size,
    gain_ref,
    lengths_ref,
    wanted_ref,
    queries_hbm,
    keys_hbm,
    values_hbm,
    residual_hbm,
    weight_hbm,
    queue_hbm,
    anchors_ref,
    losses_ref,
    q_own,
    kv_own,
    v_t,
    q_near,
    q_far,
    kv_first,
    v_t_first,
    mix_own,
    log_own,
    near_out,
    near_out_log,
    far_out,
    far_out_log,
    near_in,
    near_in_log,
    far_in,
    far_in_log,
    att_t,
    residual,
    weight,
    hidden,
    member,
    queue,
    parts,
    parts_in,
    logits,
    load_sem,
    send_sem,
    asked_sem,
    given_sem,
    part_sem,
    queue_send,
    queue_recv,
    beside_recv,
):
    chunks, tok_rows, chunk_cols = q_own.shape
    heads = chunk_cols // head_size
    own_rows, width = anchors_ref.shape
    funcs = own_rows * n_seq
    pieces, piece_rows = queue.shape[1:3]
    queue_rows = pieces * piece_rows
    seq = lax.axis_index("seq")
    batch = lax.axis_index("batch")

    pair = near_out_log.shape[1]

    def start_loads(g, carry):
        cols = pl.ds(pl.multiple_of(g * chunk_cols, chunk_cols), chunk_cols)
        pltpu.make_async_copy(queries_hbm.at[:, cols], q_own.at[g], load_sem.at[0]).start()
        pltpu.make_async_copy(keys_hbm.at[:, cols], kv_own.at[g, 0], load_sem.at[1]).start()
        pltpu.make_async_copy(values_hbm.at[:, cols], kv_own.at[g, 1], load_sem.at[1]).start()
        return carry

    lax.fori_loop(0, chunks, start_loads, 0)
    queue_load = pltpu.make_async_copy(queue_hbm, queue.at[batch], load_sem.at[2])
    residual_load = pltpu.make_async_copy(residual_hbm, residual, load_sem.at[3])
    weight_load = pltpu.make_async_copy(weight_hbm, weight, load_sem.at[4])
    queue_load.start()
    residual_load.start()
    weight_load.start()

    core = lax.rem(batch, 2)
    row = lax.rem(batch // 2, 2)
    col = batch // 4
    n_col = n_batch // 4

    def shard_at(c, r, k):
        return (c * 2 + r) * 2 + k

    cols_away = [lax.rem(col + d, n_col) for d in range(1, n_col)]
    sibling = shard_at(col, row, 1 - core)
    across = shard_at(col, 1 - row, core)
    along = [shard_at(c, row, core) for c in cols_away]
    diagonal = [shard_at(c, 1 - row, core) for c in cols_away]
    queue_peers = [sibling, across] + along

    seq_peers = [lax.rem(seq + d, n_seq) for d in range(1, n_seq)]
    barrier = pltpu.get_barrier_semaphore()
    for peer in seq_peers:
        pl.semaphore_signal(barrier, inc=1, device_id={"seq": peer}, device_id_type=MESH)
    for peer in queue_peers:
        pl.semaphore_signal(barrier, inc=1, device_id={"batch": peer}, device_id_type=MESH)
    pl.semaphore_wait(barrier, n_seq - 1 + len(queue_peers))

    is_first = seq == 0
    is_second = seq == 1
    later = seq >= 2
    has_near = seq <= n_seq - 2

    left, left_two = lax.rem(seq + n_seq - 1, n_seq), lax.rem(seq + n_seq - 2, n_seq)
    right, right_two = lax.rem(seq + 1, n_seq), lax.rem(seq + 2, n_seq)

    def remote(kind, source, target, recv_sem, peer):
        return pltpu.make_async_remote_copy(
            src_ref=source,
            dst_ref=target,
            send_sem=send_sem.at[kind],
            recv_sem=recv_sem,
            device_id={"seq": peer},
            device_id_type=MESH,
        )

    def ask_near(g):
        return remote(0, q_own.at[g], q_near.at[g], asked_sem.at[0, g], left)

    def ask_far(g):
        return remote(1, q_own.at[g], q_far.at[g], asked_sem.at[1, g], left_two)

    def give_first(g):
        return remote(2, kv_own.at[g], kv_first.at[g], asked_sem.at[2, g], right)

    def give_near(at, t):
        return remote(3, near_out.at[at], near_in.at[at], given_sem.at[0, t], right)

    def give_near_log(t):
        return remote(4, near_out_log.at[t], near_in_log.at[t], given_sem.at[1, t], right)

    def give_far(at, t):
        return remote(5, far_out.at[at], far_in.at[at], given_sem.at[2, t], right_two)

    def give_far_log(t):
        return remote(6, far_out_log.at[t], far_in_log.at[t], given_sem.at[3, t], right_two)

    def queue_copy(shard, k, sem, p):
        return pltpu.make_async_remote_copy(
            src_ref=queue.at[shard, k],
            dst_ref=queue.at[shard, k],
            send_sem=queue_send.at[0],
            recv_sem=sem,
            device_id={"batch": queue_peers[p]},
            device_id_type=MESH,
        )

    def spread_own(k, carry):
        queue_copy(batch, k, queue_recv.at[0, k], 1).start()
        for d in range(1, n_col):
            queue_copy(batch, k, queue_recv.at[n_col - d, k], 1 + d).start()
        queue_copy(batch, k, beside_recv.at[0], 0).start()
        return carry

    def forward(k):
        for e, shard in enumerate([across] + along):
            queue_copy(shard, k, queue_recv.at[e, k], 1).wait_recv()

        @pl.when(lax.rem(k, 2) == 0)
        def _():
            for d in range(1, n_col):
                sem = queue_recv.at[n_col - 1 + n_col - d, k]
                queue_copy(across, k, sem, 1 + d).start()

        @pl.when(lax.rem(k, 2) == 1)
        def _():
            for e in range(1, n_col):
                queue_copy(along[e - 1], k, queue_recv.at[n_col - 1 + e, k], 1).start()

        for shard in [across] + along:
            queue_copy(shard, k, beside_recv.at[0], 0).start()

    def forward_diagonal(k):
        for e, shard in enumerate(diagonal):
            queue_copy(shard, k, queue_recv.at[n_col + e, k], 1).wait_recv()
            queue_copy(shard, k, beside_recv.at[1], 0).start()

    pltpu.make_async_copy(q_own, q_own, load_sem.at[0]).wait()

    @pl.when(seq >= 3)
    def _():
        def ask_both(g, carry):
            ask_far(g).start()
            ask_near(g).start()
            return carry

        lax.fori_loop(0, chunks, ask_both, 0)

    @pl.when(seq == 2)
    def _():
        def ask_one(g, carry):
            ask_near(g).start()
            return carry

        lax.fori_loop(0, chunks, ask_one, 0)

    pltpu.make_async_copy(kv_own, kv_own, load_sem.at[1]).wait()

    @pl.when(is_first)
    def _():
        def give(g, carry):
            give_first(g).start()
            return carry

        lax.fori_loop(0, chunks, give, 0)

    queue_load.wait()
    lax.fori_loop(0, pieces, spread_own, 0)

    row_ids = lax.broadcasted_iota(jnp.int32, (funcs, funcs), 0)
    func_ids = lax.broadcasted_iota(jnp.int32, (funcs, funcs), 1)
    listed = lax.rem(row_ids, own_rows) * n_seq + row_ids // own_rows
    lengths = jnp.broadcast_to(lengths_ref[...].astype(F32), (funcs, funcs))
    begin_at = jnp.sum(jnp.where(func_ids < listed, lengths, 0.0), axis=1, keepdims=True)
    end_at = jnp.sum(jnp.where(func_ids <= listed, lengths, 0.0), axis=1, keepdims=True)
    pos = (
        seq * tok_rows + lax.broadcasted_iota(jnp.int32, (funcs, tok_rows), 1)
    ).astype(F32)
    member[...] = jnp.where((pos >= begin_at) & (pos < end_at), 1.0, 0.0).astype(BF16)

    def near_to(g, blocks):
        t, n = g // pair, lax.rem(g, pair)
        mixed, logs = attend(q_near[g], blocks, head_size)
        near_out_log[t, n] = logs
        near_out[g] = mixed.astype(BF16)
        give_near(g, t).start()

        @pl.when(n == pair - 1)
        def _():
            give_near_log(t).start()

    def far_to(g):
        t, n = g // pair, lax.rem(g, pair)
        ask_far(g).wait_recv()
        mixed, logs = attend(q_far[g], [own_keys(g) + (2,)], head_size)
        far_out_log[t, n] = logs
        far_out[g] = mixed.astype(BF16)
        give_far(g, t).start()

        @pl.when(n == pair - 1)
        def _():
            give_far_log(t).start()

    def own_keys(g):
        return (kv_own.at[g, 0], v_t.at[g])

    def first_keys(g):
        return (kv_first.at[g, 0], v_t_first.at[g])

    def step(g, carry):
        v_t[g] = kv_own[g, 1].T

        @pl.when(is_first)
        def _():
            mixed, _ = attend(q_own[g], [own_keys(g) + (0,)], head_size)
            att_t[g] = mixed.astype(BF16)

        @pl.when(is_second)
        def _():
            far_to(g)
            give_first(g).wait_recv()
            v_t_first[g] = kv_first[g, 1].T
            ask_near(g).wait_recv()
            near_to(g, [own_keys(g) + (1,), first_keys(g) + (2,)])
            mixed, _ = attend(q_own[g], [own_keys(g) + (0,), first_keys(g) + (1,)], head_size)
            att_t[g] = mixed.astype(BF16)

        @pl.when(later & has_near)
        def _():
            ask_near(g).wait_recv()
            near_to(g, [own_keys(g) + (1,)])

        if n_seq > 4:

            @pl.when(later & (seq <= n_seq - 3))
            def _():
                far_to(g)

        @pl.when(later)
        def _():
            mixed, logs = attend(q_own[g], [own_keys(g) + (0,)], head_size)
            mix_own[g] = mixed
            log_own[g] = logs

        @pl.when((g >= 2) & (g <= 2 * pieces) & (lax.rem(g, 2) == 0))
        def _():
            forward(g // 2 - 1)

        return carry

    lax.fori_loop(0, chunks, step, 0)
    for k in range(min(chunks // 2 - 1, pieces), pieces):
        forward(k)

    residual_load.wait()
    weight_load.wait()
    hidden[...] = residual[...].astype(F32)

    def project(t, carry):
        both = pl.ds(t * pair, pair)

        @pl.when(later)
        def _():
            give_near(both, t).wait_recv()
            give_near_log(t).wait_recv()

        @pl.when(seq == 2)
        def _():
            for n in range(pair):
                g = t * pair + n
                att_t[g] = merge(
                    [(mix_own[g], log_own[g]), (near_in[g], near_in_log[t, n])], heads, head_size
                )

        @pl.when(seq >= 3)
        def _():
            give_far(both, t).wait_recv()
            give_far_log(t).wait_recv()
            for n in range(pair):
                g = t * pair + n
                att_t[g] = merge(
                    [
                        (mix_own[g], log_own[g]),
                        (near_in[g], near_in_log[t, n]),
                        (far_in[g], far_in_log[t, n]),
                    ],
                    heads,
                    head_size,
                )

        depth = pair * chunk_cols
        hidden[...] += lax.dot_general(
            att_t[both].reshape(depth, tok_rows),
            weight[pl.ds(pl.multiple_of(t * depth, depth), depth), :],
            (((0,), (0,)), ((), ())),
            preferred_element_type=F32,
        )
        return carry

    lax.fori_loop(0, chunks // pair, project, 0)

    total = hidden[...]
    scale = lax.rsqrt(jnp.mean(total * total, axis=-1, keepdims=True) + 1e-05)
    normed = (total * scale * gain_ref[...]).astype(BF16)
    partial = jnp.dot(member[...], normed, preferred_element_type=F32)
    parts[...] = partial.reshape(n_seq, own_rows, width).astype(BF16)
    def part_copy(source, target, peer):
        return pltpu.make_async_remote_copy(
            src_ref=source,
            dst_ref=target,
            send_sem=part_sem.at[0],
            recv_sem=part_sem.at[1],
            device_id={"seq": peer},
            device_id_type=MESH,
        )

    for d in range(1, n_seq):
        peer = seq_peers[d - 1]
        part_copy(parts.at[peer], parts_in.at[d - 1], peer).start()
    for k in range(pieces // 2):
        forward_diagonal(k)
    all_parts = part_copy(parts_in, parts_in, right)
    all_parts.wait_recv()
    pooled = parts[seq].astype(F32)
    for d in range(1, n_seq):
        pooled = pooled + parts_in[d - 1].astype(F32)
    anchors = (
        pooled * lax.rsqrt(jnp.sum(pooled * pooled, axis=-1, keepdims=True) + 1e-06)
    ).astype(BF16)
    anchors_ref[...] = anchors

    def logits_of(shard):
        logits[shard] = LOGIT_SCALE * lax.dot_general(
            anchors,
            queue[shard].reshape(queue_rows, width),
            ROWS_T,
            preferred_element_type=F32,
        )

    def await_beside(at, shards):
        ref = queue.at[pl.ds(0, shards)]
        pltpu.make_async_remote_copy(
            src_ref=ref,
            dst_ref=ref,
            send_sem=queue_send.at[0],
            recv_sem=beside_recv.at[at],
            device_id={"batch": sibling},
            device_id_type=MESH,
        ).wait_recv()

    for shard in [batch, across] + along:
        logits_of(shard)
    for k in range(pieces // 2, pieces):
        forward_diagonal(k)
    await_beside(0, n_col + 1)
    for shard in [sibling, shard_at(col, 1 - row, 1 - core)]:
        logits_of(shard)
    for c in cols_away:
        logits_of(shard_at(c, row, 1 - core))
    for shard in diagonal:
        logits_of(shard)
    await_beside(1, n_col - 1)
    for c in cols_away:
        logits_of(shard_at(c, 1 - row, 1 - core))

    square = (own_rows, own_rows)
    on_diagonal = lax.broadcasted_iota(jnp.int32, square, 0) == lax.broadcasted_iota(
        jnp.int32, square, 1
    )
    wanted = jnp.broadcast_to(wanted_ref[pl.ds(batch, 1), :].astype(F32), square)
    wanted = jnp.sum(jnp.where(on_diagonal, wanted, 0.0), axis=1, keepdims=True)
    wanted = wanted.astype(jnp.int32)
    peak = functools.reduce(
        jnp.maximum, [jnp.max(logits[b], axis=1, keepdims=True) for b in range(n_batch)]
    )
    lane = lax.broadcasted_iota(jnp.int32, (own_rows, queue_rows), 1)
    sums, chosen = 0.0, 0.0
    for b in range(n_batch):
        sums = sums + jnp.exp(logits[b] - peak)
        chosen = chosen + jnp.where(lane + b * queue_rows == wanted, logits[b], 0.0)
    loss = (
        peak
        + jnp.log(jnp.sum(sums, axis=1, keepdims=True))
        - jnp.sum(chosen, axis=1, keepdims=True)
    )
    losses_ref[...] = jnp.sum(
        jnp.where(on_diagonal, jnp.broadcast_to(loss, square), 0.0), axis=0, keepdims=True
    )

    all_parts.wait_send()
    sent = queue.at[pl.ds(0, n_batch - 1)]
    pltpu.make_async_remote_copy(
        src_ref=sent,
        dst_ref=sent,
        send_sem=queue_send.at[0],
        recv_sem=beside_recv.at[0],
        device_id={"batch": sibling},
        device_id_type=MESH,
    ).wait_send()

    def sent_all(kind, ref):
        remote(kind, ref, ref, given_sem.at[0, 0], right).wait_send()

    @pl.when(is_first)
    def _():
        sent_all(2, kv_own)

    @pl.when(later)
    def _():
        sent_all(0, q_own)

    @pl.when(seq >= 3)
    def _():
        sent_all(1, q_own)

    @pl.when((seq >= 1) & has_near)
    def _():
        sent_all(3, near_out)
        sent_all(4, near_out_log)

    @pl.when((seq >= 1) & (seq <= n_seq - 3))
    def _():
        sent_all(5, far_out)
        sent_all(6, far_out_log)


def body(
    queries, keys, values, residual, out_weight, norm_gain, source_queue, span_lengths, positives
):
    tok_rows, width = queries.shape[1:]
    head_size = width // HEADS
    n_seq = lax.axis_size("seq")
    n_batch = lax.axis_size("batch")
    own_rows = positives.shape[1]
    queue_rows = source_queue.shape[0]
    chunk_cols = 128
    chunks = width // chunk_cols
    pieces = max(2, 32 // n_batch)
    pair = 2
    piece_rows = queue_rows // pieces
    assert (WINDOW - 1) // tok_rows + 1 == 2 and chunk_cols % head_size == 0
    assert n_seq >= 4 and n_batch % 4 == 0 and pieces % 2 == 0 and piece_rows % 16 == 0
    vmem = pl.BlockSpec(memory_space=pltpu.VMEM)
    hbm = pl.BlockSpec(memory_space=pl.ANY)
    rows_bf16 = pltpu.VMEM((chunks, tok_rows, chunk_cols), BF16)
    cols_bf16 = pltpu.VMEM((chunks, chunk_cols, tok_rows), BF16)
    cols_f32 = pltpu.VMEM((chunks, chunk_cols, tok_rows), F32)
    log_f32 = pltpu.VMEM((chunks // pair, pair, chunk_cols // head_size, tok_rows), F32)
    kv_bf16 = pltpu.VMEM((chunks, 2, tok_rows, chunk_cols), BF16)
    anchors, losses = pl.pallas_call(
        functools.partial(block_kernel, n_seq, n_batch, head_size),
        out_shape=(
            jax.ShapeDtypeStruct((own_rows, width), BF16),
            jax.ShapeDtypeStruct((1, own_rows), F32),
        ),
        in_specs=[vmem] * 3 + [hbm] * 6,
        out_specs=(vmem, vmem),
        scratch_shapes=[
            rows_bf16,
            kv_bf16,
            cols_bf16,
            rows_bf16,
            rows_bf16,
            kv_bf16,
            cols_bf16,
            cols_f32,
            pltpu.VMEM((chunks, chunk_cols // head_size, tok_rows), F32),
            cols_bf16,
            log_f32,
            cols_bf16,
            log_f32,
            cols_bf16,
            log_f32,
            cols_bf16,
            log_f32,
            cols_bf16,
            pltpu.VMEM((tok_rows, width), BF16),
            pltpu.VMEM(out_weight.shape, BF16),
            pltpu.VMEM((tok_rows, width), F32),
            pltpu.VMEM((own_rows * n_seq, tok_rows), BF16),
            pltpu.VMEM((n_batch, pieces, piece_rows, width), BF16),
            pltpu.VMEM((n_seq, own_rows, width), BF16),
            pltpu.VMEM((n_seq - 1, own_rows, width), BF16),
            pltpu.VMEM((n_batch, own_rows, queue_rows), F32),
            pltpu.SemaphoreType.DMA((5,)),
            pltpu.SemaphoreType.DMA((7,)),
            pltpu.SemaphoreType.DMA((3, chunks)),
            pltpu.SemaphoreType.DMA((4, chunks // pair)),
            pltpu.SemaphoreType.DMA((2,)),
            pltpu.SemaphoreType.DMA((1,)),
            pltpu.SemaphoreType.DMA((n_batch // 2 - 1, pieces)),
            pltpu.SemaphoreType.DMA((2,)),
        ],
        compiler_params=pltpu.CompilerParams(
            collective_id=0, has_side_effects=True, vmem_limit_bytes=67043328
        ),
        name="block",
    )(
        norm_gain.reshape(1, -1),
        span_lengths,
        positives,
        queries[0],
        keys[0],
        values[0],
        residual[0],
        out_weight,
        source_queue.reshape(pieces, piece_rows, width),
    )

    def hand_on(anchors_ref, losses_ref, anchors_out, losses_out):
        anchors_out[...] = anchors_ref[...]
        losses_out[...] = losses_ref[...]

    anchors, losses = pl.pallas_call(
        hand_on,
        out_shape=(
            jax.ShapeDtypeStruct((own_rows, width), BF16),
            jax.ShapeDtypeStruct((1, own_rows), F32),
        ),
        in_specs=[vmem] * 2,
        out_specs=(vmem, vmem),
        name="hand_on",
    )(anchors, losses)
    return (anchors[None], losses)


def solution(mesh):
    return jax.shard_map(
        body,
        mesh=mesh,
        in_specs=(
            P("batch", "seq", None),
            P("batch", "seq", None),
            P("batch", "seq", None),
            P("batch", "seq", None),
            P(),
            P(),
            P("batch", None),
            P("batch", None),
            P(None, "seq"),
        ),
        out_specs=(P("batch", "seq", None), P("batch", "seq")),
        check_vma=False,
    )
```

```python
import functools
import math

import jax
import jax.numpy as jnp
from jax import lax
from jax.experimental import pallas as pl
from jax.experimental.pallas import tpu as pltpu
from jax.sharding import PartitionSpec as P

HEADS = 16
WINDOW = 512
MESH = pl.DeviceIdType.MESH
F32 = jnp.float32
BF16 = jnp.bfloat16
LOGIT_SCALE = 20.0
NEVER = -1e30
LOOKAHEAD = 3
ROWS_T = (((1,), (1,)), ((), ()))


def attend(query_chunk, key_blocks, head_size):
    tok_rows, width = query_chunk.shape
    half = tok_rows // 2
    to_log2 = math.log2(math.e) / math.sqrt(head_size)
    heads = width // head_size
    lane = lax.broadcasted_iota(jnp.int32, (tok_rows, width), 1)
    query_less_key = lax.broadcasted_iota(jnp.int32, (half, half), 1) - lax.broadcasted_iota(
        jnp.int32, (half, half), 0
    )
    units = [(h, i) for h in range(heads) for i in range(2)]

    def spans(i):
        found = []
        for key_ref, value_t, apart in key_blocks:
            offsets = [apart * tok_rows + (i - j) * half for j in range(2)]
            seen = [j for j in range(2) if -half < offsets[j] < WINDOW + half - 1]
            found.append((key_ref, value_t, offsets, seen))
        return found

    def scores_of(h, i):
        own = (lane >= h * head_size) & (lane < (h + 1) * head_size)
        query_h = jnp.where(own, query_chunk, jnp.zeros_like(query_chunk))
        query_h = query_h[i * half : (i + 1) * half]
        return [
            lax.dot_general(
                key_ref[seen[0] * half : (seen[-1] + 1) * half, :],
                query_h,
                ROWS_T,
                preferred_element_type=F32,
            )
            for key_ref, _, _, seen in spans(i)
        ]

    def finish(h, i, scores):
        blocks = []
        for (_, _, offsets, seen), score in zip(spans(i), scores):
            parts = []
            for j in seen:
                part = score[(j - seen[0]) * half : (j - seen[0] + 1) * half]
                if offsets[j] < half - 1:
                    part = jnp.where(query_less_key >= -offsets[j], part, NEVER)
                if offsets[j] + half - 1 >= WINDOW:
                    part = jnp.where(query_less_key < WINDOW - offsets[j], part, NEVER)
                parts.append(part)
            blocks.append(parts)
        peak = functools.reduce(
            jnp.maximum,
            [jnp.max(part, axis=0, keepdims=True) for parts in blocks for part in parts],
        )
        blocks = [[jnp.exp2((part - peak) * to_log2) for part in parts] for parts in blocks]
        total = sum(jnp.sum(part, axis=0, keepdims=True) for parts in blocks for part in parts)
        mixed = sum(
            jnp.dot(
                value_t[
                    h * head_size : (h + 1) * head_size, seen[0] * half : (seen[-1] + 1) * half
                ],
                jnp.concatenate([part.astype(BF16) for part in parts], axis=0),
                preferred_element_type=F32,
            )
            for (_, value_t, _, seen), parts in zip(spans(i), blocks)
        )
        return mixed * (1.0 / total), peak * to_log2 + jnp.log2(total)

    pending, results = {}, {}
    for u in range(len(units) + LOOKAHEAD):
        if u < len(units):
            pending[u] = scores_of(*units[u])
        if u >= LOOKAHEAD:
            at = u - LOOKAHEAD
            results[units[at]] = finish(*units[at], pending.pop(at))
    mixed = jnp.concatenate(
        [jnp.concatenate([results[h, i][0] for i in range(2)], axis=1) for h in range(heads)],
        axis=0,
    )
    logs = jnp.concatenate(
        [jnp.concatenate([results[h, i][1] for i in range(2)], axis=1) for h in range(heads)],
        axis=0,
    )
    return mixed, logs


def merge(parts, heads, head_size):
    mixed = []
    for h in range(heads):
        logs = [log[h : h + 1] for _, log in parts]
        top = functools.reduce(jnp.maximum, logs)
        shares = [jnp.exp2(log - top) for log in logs]
        scale = 1.0 / sum(shares)
        rows = slice(h * head_size, (h + 1) * head_size)
        mixed.append(sum(mix[rows].astype(F32) * (s * scale) for (mix, _), s in zip(parts, shares)))
    return jnp.concatenate(mixed, axis=0).astype(BF16)


def block_kernel(
    n_seq,
    n_batch,
    head_size,
    gain_ref,
    lengths_ref,
    wanted_ref,
    queries_hbm,
    keys_hbm,
    values_hbm,
    residual_hbm,
    weight_hbm,
    queue_hbm,
    anchors_ref,
    losses_ref,
    q_own,
    kv_own,
    v_t,
    q_near,
    q_far,
    kv_first,
    v_t_first,
    mix_own,
    log_own,
    near_out,
    near_out_log,
    far_out,
    far_out_log,
    near_in,
    near_in_log,
    far_in,
    far_in_log,
    att_t,
    residual,
    weight,
    hidden,
    member,
    queue,
    parts,
    parts_in,
    logits,
    load_sem,
    send_sem,
    asked_sem,
    given_sem,
    part_sem,
    queue_send,
    queue_recv,
    beside_recv,
    higher_sem,
):
    chunks, tok_rows, chunk_cols = q_own.shape
    heads = chunk_cols // head_size
    own_rows, width = anchors_ref.shape
    funcs = own_rows * n_seq
    pieces, piece_rows = queue.shape[1:3]
    queue_rows = pieces * piece_rows
    seq = lax.axis_index("seq")
    batch = lax.axis_index("batch")

    pair = near_out_log.shape[1]
    early = pair

    def start_loads(g, carry):
        cols = pl.ds(pl.multiple_of(g * chunk_cols, chunk_cols), chunk_cols)
        pltpu.make_async_copy(queries_hbm.at[:, cols], q_own.at[g], load_sem.at[0]).start()
        pltpu.make_async_copy(keys_hbm.at[:, cols], kv_own.at[g, 0], load_sem.at[1]).start()
        pltpu.make_async_copy(values_hbm.at[:, cols], kv_own.at[g, 1], load_sem.at[1]).start()
        return carry

    lax.fori_loop(0, chunks, start_loads, 0)
    queue_load = pltpu.make_async_copy(queue_hbm, queue.at[batch], load_sem.at[2])
    residual_load = pltpu.make_async_copy(residual_hbm, residual, load_sem.at[3])
    weight_load = pltpu.make_async_copy(weight_hbm, weight, load_sem.at[4])
    queue_load.start()
    residual_load.start()
    weight_load.start()

    core = lax.rem(batch, 2)
    row = lax.rem(batch // 2, 2)
    col = batch // 4
    n_col = n_batch // 4

    def shard_at(c, r, k):
        return (c * 2 + r) * 2 + k

    cols_away = [lax.rem(col + d, n_col) for d in range(1, n_col)]
    sibling = shard_at(col, row, 1 - core)
    across = shard_at(col, 1 - row, core)
    along = [shard_at(c, row, core) for c in cols_away]
    diagonal = [shard_at(c, 1 - row, core) for c in cols_away]
    queue_peers = [sibling, across] + along

    seq_peers = [lax.rem(seq + d, n_seq) for d in range(1, n_seq)]
    barrier = pltpu.get_barrier_semaphore()
    for d in range(1, n_seq):

        @pl.when(seq + d < n_seq)
        def _():
            pl.semaphore_signal(
                barrier, inc=1, device_id={"seq": seq_peers[d - 1]}, device_id_type=MESH
            )

    @pl.when(seq >= 1)
    def _():
        pl.semaphore_signal(barrier, inc=1, device_id={"seq": seq_peers[-1]}, device_id_type=MESH)

    for peer in queue_peers:
        pl.semaphore_signal(barrier, inc=1, device_id={"batch": peer}, device_id_type=MESH)
    for at in range(n_seq):

        @pl.when(seq == at)
        def _():
            pl.semaphore_wait(barrier, at + (at < n_seq - 1) + len(queue_peers))

    def tell_left():
        pl.semaphore_signal(
            higher_sem, inc=1, device_id={"seq": seq_peers[-1]}, device_id_type=MESH
        )

    @pl.when(seq == n_seq - 2)
    def _():
        tell_left()

    def hear_of_higher():
        pl.semaphore_wait(higher_sem, 1)

        @pl.when(seq >= 1)
        def _():
            tell_left()

    is_first = seq == 0
    is_second = seq == 1
    later = seq >= 2
    has_near = seq <= n_seq - 2

    left, left_two = lax.rem(seq + n_seq - 1, n_seq), lax.rem(seq + n_seq - 2, n_seq)
    right, right_two = lax.rem(seq + 1, n_seq), lax.rem(seq + 2, n_seq)

    def remote(kind, source, target, recv_sem, peer):
        return pltpu.make_async_remote_copy(
            src_ref=source,
            dst_ref=target,
            send_sem=send_sem.at[kind],
            recv_sem=recv_sem,
            device_id={"seq": peer},
            device_id_type=MESH,
        )

    def ask_near(g):
        return remote(0, q_own.at[g], q_near.at[g], asked_sem.at[0, g], left)

    def ask_far(g):
        return remote(1, q_own.at[g], q_far.at[g], asked_sem.at[1, g], left_two)

    def give_first(g):
        return remote(2, kv_own.at[g], kv_first.at[g], asked_sem.at[2, g], right)

    def give_near(at, t):
        return remote(3, near_out.at[at], near_in.at[at], given_sem.at[0, t], right)

    def give_near_log(t):
        return remote(4, near_out_log.at[t], near_in_log.at[t], given_sem.at[1, t], right)

    def give_far(at, t):
        return remote(5, far_out.at[at], far_in.at[at], given_sem.at[2, t], right_two)

    def give_far_log(t):
        return remote(6, far_out_log.at[t], far_in_log.at[t], given_sem.at[3, t], right_two)

    def queue_copy(shard, k, sem, p):
        return pltpu.make_async_remote_copy(
            src_ref=queue.at[shard, k],
            dst_ref=queue.at[shard, k],
            send_sem=queue_send.at[0],
            recv_sem=sem,
            device_id={"batch": queue_peers[p]},
            device_id_type=MESH,
        )

    def spread_own(k, carry):
        queue_copy(batch, k, queue_recv.at[0, k], 1).start()
        for d in range(1, n_col):
            queue_copy(batch, k, queue_recv.at[n_col - d, k], 1 + d).start()
        queue_copy(batch, k, beside_recv.at[0], 0).start()
        return carry

    def forward(k):
        for e, shard in enumerate([across] + along):
            queue_copy(shard, k, queue_recv.at[e, k], 1).wait_recv()

        @pl.when(lax.rem(k, 2) == 0)
        def _():
            for d in range(1, n_col):
                sem = queue_recv.at[n_col - 1 + n_col - d, k]
                queue_copy(across, k, sem, 1 + d).start()

        @pl.when(lax.rem(k, 2) == 1)
        def _():
            for e in range(1, n_col):
                queue_copy(along[e - 1], k, queue_recv.at[n_col - 1 + e, k], 1).start()

        for shard in [across] + along:
            queue_copy(shard, k, beside_recv.at[0], 0).start()

    def forward_diagonal(k):
        for e, shard in enumerate(diagonal):
            queue_copy(shard, k, queue_recv.at[n_col + e, k], 1).wait_recv()
            queue_copy(shard, k, beside_recv.at[1], 0).start()

    pltpu.make_async_copy(q_own, q_own, load_sem.at[0]).wait()

    @pl.when(seq >= 3)
    def _():
        def ask_both(g, carry):
            @pl.when((seq > 3) | (g >= early))
            def _():
                ask_far(g).start()

            ask_near(g).start()
            return carry

        lax.fori_loop(0, chunks, ask_both, 0)

    @pl.when(seq == 2)
    def _():
        def ask_one(g, carry):
            ask_near(g).start()
            return carry

        lax.fori_loop(0, chunks, ask_one, 0)

    pltpu.make_async_copy(kv_own, kv_own, load_sem.at[1]).wait()

    @pl.when(is_first)
    def _():
        def give(g, carry):
            give_first(g).start()
            return carry

        lax.fori_loop(0, chunks, give, 0)

    @pl.when(is_second)
    def _():
        for g in range(early):
            give_first(g).start()

    queue_load.wait()
    lax.fori_loop(0, pieces, spread_own, 0)

    row_ids = lax.broadcasted_iota(jnp.int32, (funcs, funcs), 0)
    func_ids = lax.broadcasted_iota(jnp.int32, (funcs, funcs), 1)
    listed = lax.rem(row_ids, own_rows) * n_seq + row_ids // own_rows
    lengths = jnp.broadcast_to(lengths_ref[...].astype(F32), (funcs, funcs))
    begin_at = jnp.sum(jnp.where(func_ids < listed, lengths, 0.0), axis=1, keepdims=True)
    end_at = jnp.sum(jnp.where(func_ids <= listed, lengths, 0.0), axis=1, keepdims=True)
    pos = (
        seq * tok_rows + lax.broadcasted_iota(jnp.int32, (funcs, tok_rows), 1)
    ).astype(F32)
    member[...] = jnp.where((pos >= begin_at) & (pos < end_at), 1.0, 0.0).astype(BF16)

    def near_to(g, blocks):
        t, n = g // pair, lax.rem(g, pair)
        mixed, logs = attend(q_near[g], blocks, head_size)
        near_out_log[t, n] = logs
        near_out[g] = mixed.astype(BF16)
        give_near(g, t).start()

        @pl.when(n == pair - 1)
        def _():
            give_near_log(t).start()

    def far_to(g):
        t, n = g // pair, lax.rem(g, pair)
        ask_far(g).wait_recv()
        mixed, logs = attend(q_far[g], [own_keys(g) + (2,)], head_size)
        far_out_log[t, n] = logs
        far_out[g] = mixed.astype(BF16)
        give_far(g, t).start()

        @pl.when(n == pair - 1)
        def _():
            give_far_log(t).start()

    def own_keys(g):
        return (kv_own.at[g, 0], v_t.at[g])

    def first_keys(g):
        return (kv_first.at[g, 0], v_t_first.at[g])

    def await_first(g):
        give_first(g).wait_recv()
        v_t_first[g] = kv_first[g, 1].T

    if n_seq > 4:

        @pl.when((seq >= 2) & (seq <= n_seq - 3))
        def _():
            hear_of_higher()

    def step(g, carry):
        v_t[g] = kv_own[g, 1].T

        @pl.when(is_first)
        def _():
            mixed, _ = attend(q_own[g], [own_keys(g) + (0,)], head_size)
            att_t[g] = mixed.astype(BF16)

        @pl.when(is_second & (g < early))
        def _():
            await_first(g)
            ask_near(g).wait_recv()
            near_to(g, [first_keys(g) + (2,)])

        @pl.when(is_second & (g >= early))
        def _():
            far_to(g)
            await_first(g)
            ask_near(g).wait_recv()
            near_to(g, [own_keys(g) + (1,), first_keys(g) + (2,)])

        @pl.when(is_second)
        def _():
            mixed, _ = attend(q_own[g], [own_keys(g) + (0,), first_keys(g) + (1,)], head_size)
            att_t[g] = mixed.astype(BF16)

        third = (seq == 2) & (g < early)

        @pl.when(third)
        def _():
            await_first(g)
            ask_near(g).wait_recv()
            near_to(g, [own_keys(g) + (1,), first_keys(g) + (2,)])
            mixed, logs = attend(q_own[g], [own_keys(g) + (0,), first_keys(g) + (1,)], head_size)
            mix_own[g] = mixed
            log_own[g] = logs

        @pl.when(later & has_near & jnp.logical_not(third))
        def _():
            ask_near(g).wait_recv()
            near_to(g, [own_keys(g) + (1,)])

        if n_seq > 4:

            @pl.when(later & (seq <= n_seq - 3))
            def _():
                far_to(g)

        @pl.when(later & jnp.logical_not(third))
        def _():
            mixed, logs = attend(q_own[g], [own_keys(g) + (0,)], head_size)
            mix_own[g] = mixed
            log_own[g] = logs

        @pl.when((g == early - 1) & (seq <= 1))
        def _():
            hear_of_higher()

        @pl.when((g >= 2) & (g <= 2 * pieces) & (lax.rem(g, 2) == 0))
        def _():
            forward(g // 2 - 1)

        return carry

    lax.fori_loop(0, chunks, step, 0)
    for k in range(min(chunks // 2 - 1, pieces), pieces):
        forward(k)

    residual_load.wait()
    weight_load.wait()
    hidden[...] = residual[...].astype(F32)

    def project(t, carry):
        both = pl.ds(t * pair, pair)

        @pl.when(later)
        def _():
            give_near(both, t).wait_recv()
            give_near_log(t).wait_recv()

        @pl.when((seq == 2) | ((seq == 3) & (t == 0)))
        def _():
            for n in range(pair):
                g = t * pair + n
                att_t[g] = merge(
                    [(mix_own[g], log_own[g]), (near_in[g], near_in_log[t, n])], heads, head_size
                )

        @pl.when((seq > 3) | ((seq == 3) & (t > 0)))
        def _():
            give_far(both, t).wait_recv()
            give_far_log(t).wait_recv()
            for n in range(pair):
                g = t * pair + n
                att_t[g] = merge(
                    [
                        (mix_own[g], log_own[g]),
                        (near_in[g], near_in_log[t, n]),
                        (far_in[g], far_in_log[t, n]),
                    ],
                    heads,
                    head_size,
                )

        depth = pair * chunk_cols
        hidden[...] += lax.dot_general(
            att_t[both].reshape(depth, tok_rows),
            weight[pl.ds(pl.multiple_of(t * depth, depth), depth), :],
            (((0,), (0,)), ((), ())),
            preferred_element_type=F32,
        )
        return carry

    lax.fori_loop(0, chunks // pair, project, 0)

    total = hidden[...]
    scale = lax.rsqrt(jnp.mean(total * total, axis=-1, keepdims=True) + 1e-05)
    normed = (total * scale * gain_ref[...]).astype(BF16)
    partial = jnp.dot(member[...], normed, preferred_element_type=F32)
    parts[...] = partial.reshape(n_seq, own_rows, width).astype(BF16)
    def part_copy(source, target, peer):
        return pltpu.make_async_remote_copy(
            src_ref=source,
            dst_ref=target,
            send_sem=part_sem.at[0],
            recv_sem=part_sem.at[1],
            device_id={"seq": peer},
            device_id_type=MESH,
        )

    for d in range(1, n_seq):
        peer = seq_peers[d - 1]
        part_copy(parts.at[peer], parts_in.at[d - 1], peer).start()
    for k in range(pieces // 2):
        forward_diagonal(k)
    all_parts = part_copy(parts_in, parts_in, right)
    all_parts.wait_recv()
    pooled = parts[seq].astype(F32)
    for d in range(1, n_seq):
        pooled = pooled + parts_in[d - 1].astype(F32)
    anchors = (
        pooled * lax.rsqrt(jnp.sum(pooled * pooled, axis=-1, keepdims=True) + 1e-06)
    ).astype(BF16)
    anchors_ref[...] = anchors

    def logits_of(shard):
        logits[shard] = LOGIT_SCALE * lax.dot_general(
            anchors,
            queue[shard].reshape(queue_rows, width),
            ROWS_T,
            preferred_element_type=F32,
        )

    def await_beside(at, shards):
        ref = queue.at[pl.ds(0, shards)]
        pltpu.make_async_remote_copy(
            src_ref=ref,
            dst_ref=ref,
            send_sem=queue_send.at[0],
            recv_sem=beside_recv.at[at],
            device_id={"batch": sibling},
            device_id_type=MESH,
        ).wait_recv()

    for shard in [batch, across] + along:
        logits_of(shard)
    for k in range(pieces // 2, pieces):
        forward_diagonal(k)
    await_beside(0, n_col + 1)
    for shard in [sibling, shard_at(col, 1 - row, 1 - core)]:
        logits_of(shard)
    for c in cols_away:
        logits_of(shard_at(c, row, 1 - core))
    for shard in diagonal:
        logits_of(shard)
    await_beside(1, n_col - 1)
    for c in cols_away:
        logits_of(shard_at(c, 1 - row, 1 - core))

    square = (own_rows, own_rows)
    on_diagonal = lax.broadcasted_iota(jnp.int32, square, 0) == lax.broadcasted_iota(
        jnp.int32, square, 1
    )
    wanted = jnp.broadcast_to(wanted_ref[pl.ds(batch, 1), :].astype(F32), square)
    wanted = jnp.sum(jnp.where(on_diagonal, wanted, 0.0), axis=1, keepdims=True)
    wanted = wanted.astype(jnp.int32)
    peak = functools.reduce(
        jnp.maximum, [jnp.max(logits[b], axis=1, keepdims=True) for b in range(n_batch)]
    )
    lane = lax.broadcasted_iota(jnp.int32, (own_rows, queue_rows), 1)
    sums, chosen = 0.0, 0.0
    for b in range(n_batch):
        sums = sums + jnp.exp(logits[b] - peak)
        chosen = chosen + jnp.where(lane + b * queue_rows == wanted, logits[b], 0.0)
    loss = (
        peak
        + jnp.log(jnp.sum(sums, axis=1, keepdims=True))
        - jnp.sum(chosen, axis=1, keepdims=True)
    )
    losses_ref[...] = jnp.sum(
        jnp.where(on_diagonal, jnp.broadcast_to(loss, square), 0.0), axis=0, keepdims=True
    )

    all_parts.wait_send()
    sent = queue.at[pl.ds(0, n_batch - 1)]
    pltpu.make_async_remote_copy(
        src_ref=sent,
        dst_ref=sent,
        send_sem=queue_send.at[0],
        recv_sem=beside_recv.at[0],
        device_id={"batch": sibling},
        device_id_type=MESH,
    ).wait_send()

    def sent_all(kind, ref):
        remote(kind, ref, ref, given_sem.at[0, 0], right).wait_send()

    @pl.when(is_first)
    def _():
        sent_all(2, kv_own)

    @pl.when(later)
    def _():
        sent_all(0, q_own)

    late = pl.ds(early, chunks - early)

    @pl.when(is_second)
    def _():
        sent_all(2, kv_own.at[pl.ds(0, early)])

    @pl.when(seq == 3)
    def _():
        sent_all(1, q_own.at[late])

    @pl.when(seq > 3)
    def _():
        sent_all(1, q_own)

    @pl.when((seq >= 1) & has_near)
    def _():
        sent_all(3, near_out)
        sent_all(4, near_out_log)

    @pl.when(is_second)
    def _():
        sent_all(5, far_out.at[late])
        sent_all(6, far_out_log.at[pl.ds(1, chunks // pair - 1)])

    if n_seq > 4:

        @pl.when(later & (seq <= n_seq - 3))
        def _():
            sent_all(5, far_out)
            sent_all(6, far_out_log)


def body(
    queries, keys, values, residual, out_weight, norm_gain, source_queue, span_lengths, positives
):
    tok_rows, width = queries.shape[1:]
    head_size = width // HEADS
    n_seq = lax.axis_size("seq")
    n_batch = lax.axis_size("batch")
    own_rows = positives.shape[1]
    queue_rows = source_queue.shape[0]
    chunk_cols = 128
    chunks = width // chunk_cols
    pieces = max(2, 32 // n_batch)
    pair = 2
    piece_rows = queue_rows // pieces
    assert (WINDOW - 1) // tok_rows + 1 == 2 and chunk_cols % head_size == 0
    assert n_seq >= 4 and n_batch % 4 == 0 and pieces % 2 == 0 and piece_rows % 16 == 0
    vmem = pl.BlockSpec(memory_space=pltpu.VMEM)
    hbm = pl.BlockSpec(memory_space=pl.ANY)
    rows_bf16 = pltpu.VMEM((chunks, tok_rows, chunk_cols), BF16)
    cols_bf16 = pltpu.VMEM((chunks, chunk_cols, tok_rows), BF16)
    cols_f32 = pltpu.VMEM((chunks, chunk_cols, tok_rows), F32)
    log_f32 = pltpu.VMEM((chunks // pair, pair, chunk_cols // head_size, tok_rows), F32)
    kv_bf16 = pltpu.VMEM((chunks, 2, tok_rows, chunk_cols), BF16)
    anchors, losses = pl.pallas_call(
        functools.partial(block_kernel, n_seq, n_batch, head_size),
        out_shape=(
            jax.ShapeDtypeStruct((own_rows, width), BF16),
            jax.ShapeDtypeStruct((1, own_rows), F32),
        ),
        in_specs=[vmem] * 3 + [hbm] * 6,
        out_specs=(vmem, vmem),
        scratch_shapes=[
            rows_bf16,
            kv_bf16,
            cols_bf16,
            rows_bf16,
            rows_bf16,
            kv_bf16,
            cols_bf16,
            cols_f32,
            pltpu.VMEM((chunks, chunk_cols // head_size, tok_rows), F32),
            cols_bf16,
            log_f32,
            cols_bf16,
            log_f32,
            cols_bf16,
            log_f32,
            cols_bf16,
            log_f32,
            cols_bf16,
            pltpu.VMEM((tok_rows, width), BF16),
            pltpu.VMEM(out_weight.shape, BF16),
            pltpu.VMEM((tok_rows, width), F32),
            pltpu.VMEM((own_rows * n_seq, tok_rows), BF16),
            pltpu.VMEM((n_batch, pieces, piece_rows, width), BF16),
            pltpu.VMEM((n_seq, own_rows, width), BF16),
            pltpu.VMEM((n_seq - 1, own_rows, width), BF16),
            pltpu.VMEM((n_batch, own_rows, queue_rows), F32),
            pltpu.SemaphoreType.DMA((5,)),
            pltpu.SemaphoreType.DMA((7,)),
            pltpu.SemaphoreType.DMA((3, chunks)),
            pltpu.SemaphoreType.DMA((4, chunks // pair)),
            pltpu.SemaphoreType.DMA((2,)),
            pltpu.SemaphoreType.DMA((1,)),
            pltpu.SemaphoreType.DMA((n_batch // 2 - 1, pieces)),
            pltpu.SemaphoreType.DMA((2,)),
            pltpu.SemaphoreType.REGULAR,
        ],
        compiler_params=pltpu.CompilerParams(
            collective_id=0, has_side_effects=True, vmem_limit_bytes=67043328
        ),
        name="block",
    )(
        norm_gain.reshape(1, -1),
        span_lengths,
        positives,
        queries[0],
        keys[0],
        values[0],
        residual[0],
        out_weight,
        source_queue.reshape(pieces, piece_rows, width),
    )

    def hand_on(anchors_ref, losses_ref, anchors_out, losses_out):
        anchors_out[...] = anchors_ref[...]
        losses_out[...] = losses_ref[...]

    anchors, losses = pl.pallas_call(
        hand_on,
        out_shape=(
            jax.ShapeDtypeStruct((own_rows, width), BF16),
            jax.ShapeDtypeStruct((1, own_rows), F32),
        ),
        in_specs=[vmem] * 2,
        out_specs=(vmem, vmem),
        name="hand_on",
    )(anchors, losses)
    return (anchors[None], losses)


def solution(mesh):
    return jax.shard_map(
        body,
        mesh=mesh,
        in_specs=(
            P("batch", "seq", None),
            P("batch", "seq", None),
            P("batch", "seq", None),
            P("batch", "seq", None),
            P(),
            P(),
            P("batch", None),
            P("batch", None),
            P(None, "seq"),
        ),
        out_specs=(P("batch", "seq", None), P("batch", "seq")),
        check_vma=False,
    )
```

```python
import functools
import math

import jax
import jax.numpy as jnp
from jax import lax
from jax.experimental import pallas as pl
from jax.experimental.pallas import tpu as pltpu
from jax.sharding import PartitionSpec as P

HEADS = 16
WINDOW = 512
MESH = pl.DeviceIdType.MESH
F32 = jnp.float32
BF16 = jnp.bfloat16
LOGIT_SCALE = 20.0
NEVER = -1e30
LOOKAHEAD = 3
ROWS_T = (((1,), (1,)), ((), ()))


def attend(query_chunk, key_blocks, head_size):
    tok_rows, width = query_chunk.shape
    half = tok_rows // 2
    to_log2 = math.log2(math.e) / math.sqrt(head_size)
    heads = width // head_size
    lane = lax.broadcasted_iota(jnp.int32, (tok_rows, width), 1)
    query_less_key = lax.broadcasted_iota(jnp.int32, (half, half), 1) - lax.broadcasted_iota(
        jnp.int32, (half, half), 0
    )
    units = [(h, i) for h in range(heads) for i in range(2)]

    def spans(i):
        found = []
        for key_ref, value_t, apart in key_blocks:
            offsets = [apart * tok_rows + (i - j) * half for j in range(2)]
            seen = [j for j in range(2) if -half < offsets[j] < WINDOW + half - 1]
            found.append((key_ref, value_t, offsets, seen))
        return found

    def scores_of(h, i):
        own = (lane >= h * head_size) & (lane < (h + 1) * head_size)
        query_h = jnp.where(own, query_chunk, jnp.zeros_like(query_chunk))
        query_h = query_h[i * half : (i + 1) * half]
        return [
            lax.dot_general(
                key_ref[seen[0] * half : (seen[-1] + 1) * half, :],
                query_h,
                ROWS_T,
                preferred_element_type=F32,
            )
            for key_ref, _, _, seen in spans(i)
        ]

    def finish(h, i, scores):
        blocks = []
        for (_, _, offsets, seen), score in zip(spans(i), scores):
            parts = []
            for j in seen:
                part = score[(j - seen[0]) * half : (j - seen[0] + 1) * half]
                if offsets[j] < half - 1:
                    part = jnp.where(query_less_key >= -offsets[j], part, NEVER)
                if offsets[j] + half - 1 >= WINDOW:
                    part = jnp.where(query_less_key < WINDOW - offsets[j], part, NEVER)
                parts.append(part)
            blocks.append(parts)
        peak = functools.reduce(
            jnp.maximum,
            [jnp.max(part, axis=0, keepdims=True) for parts in blocks for part in parts],
        )
        blocks = [[jnp.exp2((part - peak) * to_log2) for part in parts] for parts in blocks]
        total = sum(jnp.sum(part, axis=0, keepdims=True) for parts in blocks for part in parts)
        mixed = sum(
            jnp.dot(
                value_t[
                    h * head_size : (h + 1) * head_size, seen[0] * half : (seen[-1] + 1) * half
                ],
                jnp.concatenate([part.astype(BF16) for part in parts], axis=0),
                preferred_element_type=F32,
            )
            for (_, value_t, _, seen), parts in zip(spans(i), blocks)
        )
        return mixed * (1.0 / total), peak * to_log2 + jnp.log2(total)

    pending, results = {}, {}
    for u in range(len(units) + LOOKAHEAD):
        if u < len(units):
            pending[u] = scores_of(*units[u])
        if u >= LOOKAHEAD:
            at = u - LOOKAHEAD
            results[units[at]] = finish(*units[at], pending.pop(at))
    mixed = jnp.concatenate(
        [jnp.concatenate([results[h, i][0] for i in range(2)], axis=1) for h in range(heads)],
        axis=0,
    )
    logs = jnp.concatenate(
        [jnp.concatenate([results[h, i][1] for i in range(2)], axis=1) for h in range(heads)],
        axis=0,
    )
    return mixed, logs


def merge(parts, heads, head_size):
    mixed = []
    for h in range(heads):
        logs = [log[h : h + 1] for _, log in parts]
        top = functools.reduce(jnp.maximum, logs)
        shares = [jnp.exp2(log - top) for log in logs]
        scale = 1.0 / sum(shares)
        rows = slice(h * head_size, (h + 1) * head_size)
        mixed.append(sum(mix[rows].astype(F32) * (s * scale) for (mix, _), s in zip(parts, shares)))
    return jnp.concatenate(mixed, axis=0).astype(BF16)


def block_kernel(
    n_seq,
    n_batch,
    head_size,
    gain_ref,
    lengths_ref,
    wanted_ref,
    queries_hbm,
    keys_hbm,
    values_hbm,
    residual_hbm,
    weight_hbm,
    queue_hbm,
    anchors_ref,
    losses_ref,
    q_own,
    kv_own,
    v_t,
    q_near,
    q_far,
    kv_first,
    v_t_first,
    mix_own,
    log_own,
    near_out,
    near_out_log,
    far_out,
    far_out_log,
    near_in,
    near_in_log,
    far_in,
    far_in_log,
    att_t,
    residual,
    weight,
    hidden,
    member,
    queue,
    parts,
    parts_in,
    logits,
    load_sem,
    send_sem,
    asked_sem,
    given_sem,
    part_sem,
    queue_send,
    queue_recv,
    beside_recv,
    higher_sem,
):
    chunks, tok_rows, chunk_cols = q_own.shape
    heads = chunk_cols // head_size
    own_rows, width = anchors_ref.shape
    funcs = own_rows * n_seq
    pieces, piece_rows = queue.shape[1:3]
    queue_rows = pieces * piece_rows
    seq = lax.axis_index("seq")
    batch = lax.axis_index("batch")

    pair = near_out_log.shape[1]
    early = pair

    def start_loads(g, carry):
        cols = pl.ds(pl.multiple_of(g * chunk_cols, chunk_cols), chunk_cols)
        pltpu.make_async_copy(queries_hbm.at[:, cols], q_own.at[g], load_sem.at[0]).start()
        pltpu.make_async_copy(keys_hbm.at[:, cols], kv_own.at[g, 0], load_sem.at[1]).start()
        pltpu.make_async_copy(values_hbm.at[:, cols], kv_own.at[g, 1], load_sem.at[1]).start()
        return carry

    queue_load = pltpu.make_async_copy(queue_hbm, queue.at[batch], load_sem.at[2])
    queue_load.start()
    lax.fori_loop(0, chunks, start_loads, 0)
    residual_load = pltpu.make_async_copy(residual_hbm, residual, load_sem.at[3])
    weight_load = pltpu.make_async_copy(weight_hbm, weight, load_sem.at[4])

    core = lax.rem(batch, 2)
    row = lax.rem(batch // 2, 2)
    col = batch // 4
    n_col = n_batch // 4

    def shard_at(c, r, k):
        return (c * 2 + r) * 2 + k

    cols_away = [lax.rem(col + d, n_col) for d in range(1, n_col)]
    sibling = shard_at(col, row, 1 - core)
    across = shard_at(col, 1 - row, core)
    along = [shard_at(c, row, core) for c in cols_away]
    diagonal = [shard_at(c, 1 - row, core) for c in cols_away]
    queue_peers = [sibling, across] + along

    seq_peers = [lax.rem(seq + d, n_seq) for d in range(1, n_seq)]
    barrier = pltpu.get_barrier_semaphore()
    for d in range(1, n_seq):

        @pl.when(seq + d < n_seq)
        def _():
            pl.semaphore_signal(
                barrier, inc=1, device_id={"seq": seq_peers[d - 1]}, device_id_type=MESH
            )

    @pl.when(seq >= 1)
    def _():
        pl.semaphore_signal(barrier, inc=1, device_id={"seq": seq_peers[-1]}, device_id_type=MESH)

    for peer in queue_peers:
        pl.semaphore_signal(barrier, inc=1, device_id={"batch": peer}, device_id_type=MESH)
    for at in range(n_seq):

        @pl.when(seq == at)
        def _():
            pl.semaphore_wait(barrier, at + (at < n_seq - 1) + len(queue_peers))

    def tell_left():
        pl.semaphore_signal(
            higher_sem, inc=1, device_id={"seq": seq_peers[-1]}, device_id_type=MESH
        )

    @pl.when(seq == n_seq - 2)
    def _():
        tell_left()

    def hear_of_higher():
        pl.semaphore_wait(higher_sem, 1)

        @pl.when(seq >= 1)
        def _():
            tell_left()

    is_first = seq == 0
    is_second = seq == 1
    later = seq >= 2
    has_near = seq <= n_seq - 2

    left, left_two = lax.rem(seq + n_seq - 1, n_seq), lax.rem(seq + n_seq - 2, n_seq)
    right, right_two = lax.rem(seq + 1, n_seq), lax.rem(seq + 2, n_seq)

    def remote(kind, source, target, recv_sem, peer):
        return pltpu.make_async_remote_copy(
            src_ref=source,
            dst_ref=target,
            send_sem=send_sem.at[kind],
            recv_sem=recv_sem,
            device_id={"seq": peer},
            device_id_type=MESH,
        )

    def ask_near(g):
        return remote(0, q_own.at[g], q_near.at[g], asked_sem.at[0, g], left)

    def ask_far(g):
        return remote(1, q_own.at[g], q_far.at[g], asked_sem.at[1, g], left_two)

    def give_first(g):
        return remote(2, kv_own.at[g], kv_first.at[g], asked_sem.at[2, g], right)

    def give_near(at, t):
        return remote(3, near_out.at[at], near_in.at[at], given_sem.at[0, t], right)

    def give_near_log(t):
        return remote(4, near_out_log.at[t], near_in_log.at[t], given_sem.at[1, t], right)

    def give_far(at, t):
        return remote(5, far_out.at[at], far_in.at[at], given_sem.at[2, t], right_two)

    def give_far_log(t):
        return remote(6, far_out_log.at[t], far_in_log.at[t], given_sem.at[3, t], right_two)

    def queue_copy(shard, k, sem, p):
        return pltpu.make_async_remote_copy(
            src_ref=queue.at[shard, k],
            dst_ref=queue.at[shard, k],
            send_sem=queue_send.at[0],
            recv_sem=sem,
            device_id={"batch": queue_peers[p]},
            device_id_type=MESH,
        )

    def spread_own(k, carry):
        queue_copy(batch, k, queue_recv.at[0, k], 1).start()
        for d in range(1, n_col):
            queue_copy(batch, k, queue_recv.at[n_col - d, k], 1 + d).start()
        queue_copy(batch, k, beside_recv.at[0], 0).start()
        return carry

    def forward(k):
        for e, shard in enumerate([across] + along):
            queue_copy(shard, k, queue_recv.at[e, k], 1).wait_recv()

        @pl.when(lax.rem(k, 2) == 0)
        def _():
            for d in range(1, n_col):
                sem = queue_recv.at[n_col - 1 + n_col - d, k]
                queue_copy(across, k, sem, 1 + d).start()

        @pl.when(lax.rem(k, 2) == 1)
        def _():
            for e in range(1, n_col):
                queue_copy(along[e - 1], k, queue_recv.at[n_col - 1 + e, k], 1).start()

        for shard in [across] + along:
            queue_copy(shard, k, beside_recv.at[0], 0).start()

    def forward_diagonal(k):
        for e, shard in enumerate(diagonal):
            queue_copy(shard, k, queue_recv.at[n_col + e, k], 1).wait_recv()
            queue_copy(shard, k, beside_recv.at[1], 0).start()

    queue_load.wait()
    lax.fori_loop(0, pieces, spread_own, 0)
    pltpu.make_async_copy(q_own, q_own, load_sem.at[0]).wait()

    @pl.when(seq >= 3)
    def _():
        def ask_both(g, carry):
            @pl.when((seq > 3) | (g >= early))
            def _():
                ask_far(g).start()

            ask_near(g).start()
            return carry

        lax.fori_loop(0, chunks, ask_both, 0)

    @pl.when(seq == 2)
    def _():
        def ask_one(g, carry):
            ask_near(g).start()
            return carry

        lax.fori_loop(0, chunks, ask_one, 0)

    pltpu.make_async_copy(kv_own, kv_own, load_sem.at[1]).wait()

    @pl.when(is_first)
    def _():
        def give(g, carry):
            give_first(g).start()
            return carry

        lax.fori_loop(0, chunks, give, 0)

    @pl.when(is_second)
    def _():
        for g in range(early):
            give_first(g).start()


    residual_load.start()
    weight_load.start()
    row_ids = lax.broadcasted_iota(jnp.int32, (funcs, funcs), 0)
    func_ids = lax.broadcasted_iota(jnp.int32, (funcs, funcs), 1)
    listed = lax.rem(row_ids, own_rows) * n_seq + row_ids // own_rows
    lengths = jnp.broadcast_to(lengths_ref[...].astype(F32), (funcs, funcs))
    begin_at = jnp.sum(jnp.where(func_ids < listed, lengths, 0.0), axis=1, keepdims=True)
    end_at = jnp.sum(jnp.where(func_ids <= listed, lengths, 0.0), axis=1, keepdims=True)
    pos = (
        seq * tok_rows + lax.broadcasted_iota(jnp.int32, (funcs, tok_rows), 1)
    ).astype(F32)
    member[...] = jnp.where((pos >= begin_at) & (pos < end_at), 1.0, 0.0).astype(BF16)

    def near_to(g, blocks):
        t, n = g // pair, lax.rem(g, pair)
        mixed, logs = attend(q_near[g], blocks, head_size)
        near_out_log[t, n] = logs
        near_out[g] = mixed.astype(BF16)
        give_near(g, t).start()

        @pl.when(n == pair - 1)
        def _():
            give_near_log(t).start()

    def far_to(g):
        t, n = g // pair, lax.rem(g, pair)
        ask_far(g).wait_recv()
        mixed, logs = attend(q_far[g], [own_keys(g) + (2,)], head_size)
        far_out_log[t, n] = logs
        far_out[g] = mixed.astype(BF16)
        give_far(g, t).start()

        @pl.when(n == pair - 1)
        def _():
            give_far_log(t).start()

    def own_keys(g):
        return (kv_own.at[g, 0], v_t.at[g])

    def first_keys(g):
        return (kv_first.at[g, 0], v_t_first.at[g])

    def await_first(g):
        give_first(g).wait_recv()
        v_t_first[g] = kv_first[g, 1].T

    if n_seq > 4:

        @pl.when((seq >= 2) & (seq <= n_seq - 3))
        def _():
            hear_of_higher()

    def step(g, carry):
        v_t[g] = kv_own[g, 1].T

        @pl.when(is_first)
        def _():
            mixed, _ = attend(q_own[g], [own_keys(g) + (0,)], head_size)
            att_t[g] = mixed.astype(BF16)

        @pl.when(is_second & (g < early))
        def _():
            await_first(g)
            ask_near(g).wait_recv()
            near_to(g, [first_keys(g) + (2,)])

        @pl.when(is_second & (g >= early))
        def _():
            far_to(g)
            await_first(g)
            ask_near(g).wait_recv()
            near_to(g, [own_keys(g) + (1,), first_keys(g) + (2,)])

        @pl.when(is_second)
        def _():
            mixed, _ = attend(q_own[g], [own_keys(g) + (0,), first_keys(g) + (1,)], head_size)
            att_t[g] = mixed.astype(BF16)

        third = (seq == 2) & (g < early)

        @pl.when(third)
        def _():
            await_first(g)
            ask_near(g).wait_recv()
            near_to(g, [own_keys(g) + (1,), first_keys(g) + (2,)])
            mixed, logs = attend(q_own[g], [own_keys(g) + (0,), first_keys(g) + (1,)], head_size)
            mix_own[g] = mixed
            log_own[g] = logs

        @pl.when(later & has_near & jnp.logical_not(third))
        def _():
            ask_near(g).wait_recv()
            near_to(g, [own_keys(g) + (1,)])

        if n_seq > 4:

            @pl.when(later & (seq <= n_seq - 3))
            def _():
                far_to(g)

        @pl.when(later & jnp.logical_not(third))
        def _():
            mixed, logs = attend(q_own[g], [own_keys(g) + (0,)], head_size)
            mix_own[g] = mixed
            log_own[g] = logs

        @pl.when((g == early - 1) & (seq <= 1))
        def _():
            hear_of_higher()

        @pl.when((g >= 2) & (g <= 2 * pieces) & (lax.rem(g, 2) == 0))
        def _():
            forward(g // 2 - 1)

        return carry

    lax.fori_loop(0, chunks, step, 0)
    for k in range(min(chunks // 2 - 1, pieces), pieces):
        forward(k)

    residual_load.wait()
    weight_load.wait()
    hidden[...] = residual[...].astype(F32)

    def project(t, carry):
        both = pl.ds(t * pair, pair)

        @pl.when(later)
        def _():
            give_near(both, t).wait_recv()
            give_near_log(t).wait_recv()

        @pl.when((seq == 2) | ((seq == 3) & (t == 0)))
        def _():
            for n in range(pair):
                g = t * pair + n
                att_t[g] = merge(
                    [(mix_own[g], log_own[g]), (near_in[g], near_in_log[t, n])], heads, head_size
                )

        @pl.when((seq > 3) | ((seq == 3) & (t > 0)))
        def _():
            give_far(both, t).wait_recv()
            give_far_log(t).wait_recv()
            for n in range(pair):
                g = t * pair + n
                att_t[g] = merge(
                    [
                        (mix_own[g], log_own[g]),
                        (near_in[g], near_in_log[t, n]),
                        (far_in[g], far_in_log[t, n]),
                    ],
                    heads,
                    head_size,
                )

        depth = pair * chunk_cols
        hidden[...] += lax.dot_general(
            att_t[both].reshape(depth, tok_rows),
            weight[pl.ds(pl.multiple_of(t * depth, depth), depth), :],
            (((0,), (0,)), ((), ())),
            preferred_element_type=F32,
        )
        return carry

    lax.fori_loop(0, chunks // pair, project, 0)

    total = hidden[...]
    scale = lax.rsqrt(jnp.mean(total * total, axis=-1, keepdims=True) + 1e-05)
    normed = (total * scale * gain_ref[...]).astype(BF16)
    partial = jnp.dot(member[...], normed, preferred_element_type=F32)
    parts[...] = partial.reshape(n_seq, own_rows, width).astype(BF16)
    def part_copy(source, target, peer):
        return pltpu.make_async_remote_copy(
            src_ref=source,
            dst_ref=target,
            send_sem=part_sem.at[0],
            recv_sem=part_sem.at[1],
            device_id={"seq": peer},
            device_id_type=MESH,
        )

    for d in range(1, n_seq):
        peer = seq_peers[d - 1]
        part_copy(parts.at[peer], parts_in.at[d - 1], peer).start()
    for k in range(pieces // 2):
        forward_diagonal(k)
    all_parts = part_copy(parts_in, parts_in, right)
    all_parts.wait_recv()
    pooled = parts[seq].astype(F32)
    for d in range(1, n_seq):
        pooled = pooled + parts_in[d - 1].astype(F32)
    anchors = (
        pooled * lax.rsqrt(jnp.sum(pooled * pooled, axis=-1, keepdims=True) + 1e-06)
    ).astype(BF16)
    anchors_ref[...] = anchors

    def logits_of(shard):
        logits[shard] = LOGIT_SCALE * lax.dot_general(
            anchors,
            queue[shard].reshape(queue_rows, width),
            ROWS_T,
            preferred_element_type=F32,
        )

    def await_beside(at, shards):
        ref = queue.at[pl.ds(0, shards)]
        pltpu.make_async_remote_copy(
            src_ref=ref,
            dst_ref=ref,
            send_sem=queue_send.at[0],
            recv_sem=beside_recv.at[at],
            device_id={"batch": sibling},
            device_id_type=MESH,
        ).wait_recv()

    for shard in [batch, across] + along:
        logits_of(shard)
    for k in range(pieces // 2, pieces):
        forward_diagonal(k)
    await_beside(0, n_col + 1)
    for shard in [sibling, shard_at(col, 1 - row, 1 - core)]:
        logits_of(shard)
    for c in cols_away:
        logits_of(shard_at(c, row, 1 - core))
    for shard in diagonal:
        logits_of(shard)
    await_beside(1, n_col - 1)
    for c in cols_away:
        logits_of(shard_at(c, 1 - row, 1 - core))

    square = (own_rows, own_rows)
    on_diagonal = lax.broadcasted_iota(jnp.int32, square, 0) == lax.broadcasted_iota(
        jnp.int32, square, 1
    )
    wanted = jnp.broadcast_to(wanted_ref[pl.ds(batch, 1), :].astype(F32), square)
    wanted = jnp.sum(jnp.where(on_diagonal, wanted, 0.0), axis=1, keepdims=True)
    wanted = wanted.astype(jnp.int32)
    peak = functools.reduce(
        jnp.maximum, [jnp.max(logits[b], axis=1, keepdims=True) for b in range(n_batch)]
    )
    lane = lax.broadcasted_iota(jnp.int32, (own_rows, queue_rows), 1)
    sums, chosen = 0.0, 0.0
    for b in range(n_batch):
        sums = sums + jnp.exp(logits[b] - peak)
        chosen = chosen + jnp.where(lane + b * queue_rows == wanted, logits[b], 0.0)
    loss = (
        peak
        + jnp.log(jnp.sum(sums, axis=1, keepdims=True))
        - jnp.sum(chosen, axis=1, keepdims=True)
    )
    losses_ref[...] = jnp.sum(
        jnp.where(on_diagonal, jnp.broadcast_to(loss, square), 0.0), axis=0, keepdims=True
    )

    all_parts.wait_send()
    sent = queue.at[pl.ds(0, n_batch - 1)]
    pltpu.make_async_remote_copy(
        src_ref=sent,
        dst_ref=sent,
        send_sem=queue_send.at[0],
        recv_sem=beside_recv.at[0],
        device_id={"batch": sibling},
        device_id_type=MESH,
    ).wait_send()

    def sent_all(kind, ref):
        remote(kind, ref, ref, given_sem.at[0, 0], right).wait_send()

    @pl.when(is_first)
    def _():
        sent_all(2, kv_own)

    @pl.when(later)
    def _():
        sent_all(0, q_own)

    late = pl.ds(early, chunks - early)

    @pl.when(is_second)
    def _():
        sent_all(2, kv_own.at[pl.ds(0, early)])

    @pl.when(seq == 3)
    def _():
        sent_all(1, q_own.at[late])

    @pl.when(seq > 3)
    def _():
        sent_all(1, q_own)

    @pl.when((seq >= 1) & has_near)
    def _():
        sent_all(3, near_out)
        sent_all(4, near_out_log)

    @pl.when(is_second)
    def _():
        sent_all(5, far_out.at[late])
        sent_all(6, far_out_log.at[pl.ds(1, chunks // pair - 1)])

    if n_seq > 4:

        @pl.when(later & (seq <= n_seq - 3))
        def _():
            sent_all(5, far_out)
            sent_all(6, far_out_log)


def body(
    queries, keys, values, residual, out_weight, norm_gain, source_queue, span_lengths, positives
):
    tok_rows, width = queries.shape[1:]
    head_size = width // HEADS
    n_seq = lax.axis_size("seq")
    n_batch = lax.axis_size("batch")
    own_rows = positives.shape[1]
    queue_rows = source_queue.shape[0]
    chunk_cols = 128
    chunks = width // chunk_cols
    pieces = max(2, 32 // n_batch)
    pair = 2
    piece_rows = queue_rows // pieces
    assert (WINDOW - 1) // tok_rows + 1 == 2 and chunk_cols % head_size == 0
    assert n_seq >= 4 and n_batch % 4 == 0 and pieces % 2 == 0 and piece_rows % 16 == 0
    vmem = pl.BlockSpec(memory_space=pltpu.VMEM)
    hbm = pl.BlockSpec(memory_space=pl.ANY)
    rows_bf16 = pltpu.VMEM((chunks, tok_rows, chunk_cols), BF16)
    cols_bf16 = pltpu.VMEM((chunks, chunk_cols, tok_rows), BF16)
    cols_f32 = pltpu.VMEM((chunks, chunk_cols, tok_rows), F32)
    log_f32 = pltpu.VMEM((chunks // pair, pair, chunk_cols // head_size, tok_rows), F32)
    kv_bf16 = pltpu.VMEM((chunks, 2, tok_rows, chunk_cols), BF16)
    anchors, losses = pl.pallas_call(
        functools.partial(block_kernel, n_seq, n_batch, head_size),
        out_shape=(
            jax.ShapeDtypeStruct((own_rows, width), BF16),
            jax.ShapeDtypeStruct((1, own_rows), F32),
        ),
        in_specs=[vmem] * 3 + [hbm] * 6,
        out_specs=(vmem, vmem),
        scratch_shapes=[
            rows_bf16,
            kv_bf16,
            cols_bf16,
            rows_bf16,
            rows_bf16,
            kv_bf16,
            cols_bf16,
            cols_f32,
            pltpu.VMEM((chunks, chunk_cols // head_size, tok_rows), F32),
            cols_bf16,
            log_f32,
            cols_bf16,
            log_f32,
            cols_bf16,
            log_f32,
            cols_bf16,
            log_f32,
            cols_bf16,
            pltpu.VMEM((tok_rows, width), BF16),
            pltpu.VMEM(out_weight.shape, BF16),
            pltpu.VMEM((tok_rows, width), F32),
            pltpu.VMEM((own_rows * n_seq, tok_rows), BF16),
            pltpu.VMEM((n_batch, pieces, piece_rows, width), BF16),
            pltpu.VMEM((n_seq, own_rows, width), BF16),
            pltpu.VMEM((n_seq - 1, own_rows, width), BF16),
            pltpu.VMEM((n_batch, own_rows, queue_rows), F32),
            pltpu.SemaphoreType.DMA((5,)),
            pltpu.SemaphoreType.DMA((7,)),
            pltpu.SemaphoreType.DMA((3, chunks)),
            pltpu.SemaphoreType.DMA((4, chunks // pair)),
            pltpu.SemaphoreType.DMA((2,)),
            pltpu.SemaphoreType.DMA((1,)),
            pltpu.SemaphoreType.DMA((n_batch // 2 - 1, pieces)),
            pltpu.SemaphoreType.DMA((2,)),
            pltpu.SemaphoreType.REGULAR,
        ],
        compiler_params=pltpu.CompilerParams(
            collective_id=0, has_side_effects=True, vmem_limit_bytes=67043328
        ),
        name="block",
    )(
        norm_gain.reshape(1, -1),
        span_lengths,
        positives,
        queries[0],
        keys[0],
        values[0],
        residual[0],
        out_weight,
        source_queue.reshape(pieces, piece_rows, width),
    )

    def hand_on(anchors_ref, losses_ref, anchors_out, losses_out):
        anchors_out[...] = anchors_ref[...]
        losses_out[...] = losses_ref[...]

    anchors, losses = pl.pallas_call(
        hand_on,
        out_shape=(
            jax.ShapeDtypeStruct((own_rows, width), BF16),
            jax.ShapeDtypeStruct((1, own_rows), F32),
        ),
        in_specs=[vmem] * 2,
        out_specs=(vmem, vmem),
        name="hand_on",
    )(anchors, losses)
    return (anchors[None], losses)


def solution(mesh):
    return jax.shard_map(
        body,
        mesh=mesh,
        in_specs=(
            P("batch", "seq", None),
            P("batch", "seq", None),
            P("batch", "seq", None),
            P("batch", "seq", None),
            P(),
            P(),
            P("batch", None),
            P("batch", None),
            P(None, "seq"),
        ),
        out_specs=(P("batch", "seq", None), P("batch", "seq")),
        check_vma=False,
    )
```

```python
import functools
import math

import jax
import jax.numpy as jnp
from jax import lax
from jax.experimental import pallas as pl
from jax.experimental.pallas import tpu as pltpu
from jax.sharding import PartitionSpec as P

HEADS = 16
WINDOW = 512
MESH = pl.DeviceIdType.MESH
F32 = jnp.float32
BF16 = jnp.bfloat16
LOGIT_SCALE = 20.0
NEVER = -1e30
LOOKAHEAD = 3
ROWS_T = (((1,), (1,)), ((), ()))


def attend(query_chunk, key_blocks, head_size):
    tok_rows, width = query_chunk.shape
    half = tok_rows // 2
    to_log2 = math.log2(math.e) / math.sqrt(head_size)
    heads = width // head_size
    lane = lax.broadcasted_iota(jnp.int32, (tok_rows, width), 1)
    query_less_key = lax.broadcasted_iota(jnp.int32, (half, half), 1) - lax.broadcasted_iota(
        jnp.int32, (half, half), 0
    )
    units = [(h, i) for h in range(heads) for i in range(2)]

    def spans(i):
        found = []
        for key_ref, value_t, apart in key_blocks:
            offsets = [apart * tok_rows + (i - j) * half for j in range(2)]
            seen = [j for j in range(2) if -half < offsets[j] < WINDOW + half - 1]
            found.append((key_ref, value_t, offsets, seen))
        return found

    def scores_of(h, i):
        own = (lane >= h * head_size) & (lane < (h + 1) * head_size)
        query_h = jnp.where(own, query_chunk, jnp.zeros_like(query_chunk))
        query_h = query_h[i * half : (i + 1) * half]
        return [
            lax.dot_general(
                key_ref[seen[0] * half : (seen[-1] + 1) * half, :],
                query_h,
                ROWS_T,
                preferred_element_type=F32,
            )
            for key_ref, _, _, seen in spans(i)
        ]

    def finish(h, i, scores):
        blocks = []
        for (_, _, offsets, seen), score in zip(spans(i), scores):
            parts = []
            for j in seen:
                part = score[(j - seen[0]) * half : (j - seen[0] + 1) * half]
                if offsets[j] < half - 1:
                    part = jnp.where(query_less_key >= -offsets[j], part, NEVER)
                if offsets[j] + half - 1 >= WINDOW:
                    part = jnp.where(query_less_key < WINDOW - offsets[j], part, NEVER)
                parts.append(part)
            blocks.append(parts)
        peak = functools.reduce(
            jnp.maximum,
            [jnp.max(part, axis=0, keepdims=True) for parts in blocks for part in parts],
        )
        blocks = [[jnp.exp2((part - peak) * to_log2) for part in parts] for parts in blocks]
        total = sum(jnp.sum(part, axis=0, keepdims=True) for parts in blocks for part in parts)
        mixed = sum(
            jnp.dot(
                value_t[
                    h * head_size : (h + 1) * head_size, seen[0] * half : (seen[-1] + 1) * half
                ],
                jnp.concatenate([part.astype(BF16) for part in parts], axis=0),
                preferred_element_type=F32,
            )
            for (_, value_t, _, seen), parts in zip(spans(i), blocks)
        )
        return mixed * (1.0 / total), peak * to_log2 + jnp.log2(total)

    pending, results = {}, {}
    for u in range(len(units) + LOOKAHEAD):
        if u < len(units):
            pending[u] = scores_of(*units[u])
        if u >= LOOKAHEAD:
            at = u - LOOKAHEAD
            results[units[at]] = finish(*units[at], pending.pop(at))
    mixed = jnp.concatenate(
        [jnp.concatenate([results[h, i][0] for i in range(2)], axis=1) for h in range(heads)],
        axis=0,
    )
    logs = jnp.concatenate(
        [jnp.concatenate([results[h, i][1] for i in range(2)], axis=1) for h in range(heads)],
        axis=0,
    )
    return mixed, logs


def merge(parts, heads, head_size):
    mixed = []
    for h in range(heads):
        logs = [log[h : h + 1] for _, log in parts]
        top = functools.reduce(jnp.maximum, logs)
        shares = [jnp.exp2(log - top) for log in logs]
        scale = 1.0 / sum(shares)
        rows = slice(h * head_size, (h + 1) * head_size)
        mixed.append(sum(mix[rows].astype(F32) * (s * scale) for (mix, _), s in zip(parts, shares)))
    return jnp.concatenate(mixed, axis=0).astype(BF16)


def block_kernel(
    n_seq,
    n_batch,
    head_size,
    gain_hbm,
    lengths_hbm,
    wanted_hbm,
    queries_hbm,
    keys_hbm,
    values_hbm,
    residual_hbm,
    weight_hbm,
    queue_hbm,
    anchors_ref,
    losses_ref,
    q_own,
    kv_own,
    v_t,
    q_near,
    q_far,
    kv_first,
    v_t_first,
    mix_own,
    log_own,
    near_out,
    near_out_log,
    far_out,
    far_out_log,
    near_in,
    near_in_log,
    far_in,
    far_in_log,
    att_t,
    residual,
    weight,
    hidden,
    member,
    queue,
    parts,
    parts_in,
    logits,
    load_sem,
    send_sem,
    asked_sem,
    given_sem,
    part_sem,
    queue_send,
    queue_recv,
    beside_recv,
    higher_sem,
    gain_ref,
    lengths_ref,
    wanted_ref,
):
    chunks, tok_rows, chunk_cols = q_own.shape
    heads = chunk_cols // head_size
    own_rows, width = anchors_ref.shape
    funcs = own_rows * n_seq
    pieces, piece_rows = queue.shape[1:3]
    queue_rows = pieces * piece_rows
    seq = lax.axis_index("seq")
    batch = lax.axis_index("batch")

    core = lax.rem(batch, 2)
    row = lax.rem(batch // 2, 2)
    col = batch // 4
    n_col = n_batch // 4

    def shard_at(c, r, k):
        return (c * 2 + r) * 2 + k

    cols_away = [lax.rem(col + d, n_col) for d in range(1, n_col)]
    sibling = shard_at(col, row, 1 - core)
    across = shard_at(col, 1 - row, core)
    along = [shard_at(c, row, core) for c in cols_away]
    diagonal = [shard_at(c, 1 - row, core) for c in cols_away]
    queue_peers = [sibling, across] + along

    seq_peers = [lax.rem(seq + d, n_seq) for d in range(1, n_seq)]
    barrier = pltpu.get_barrier_semaphore()
    for d in range(1, n_seq):

        @pl.when(seq + d < n_seq)
        def _():
            pl.semaphore_signal(
                barrier, inc=1, device_id={"seq": seq_peers[d - 1]}, device_id_type=MESH
            )

    @pl.when(seq >= 1)
    def _():
        pl.semaphore_signal(barrier, inc=1, device_id={"seq": seq_peers[-1]}, device_id_type=MESH)

    for peer in queue_peers:
        pl.semaphore_signal(barrier, inc=1, device_id={"batch": peer}, device_id_type=MESH)
    pair = near_out_log.shape[1]
    early = pair

    def start_loads(g, carry):
        cols = pl.ds(pl.multiple_of(g * chunk_cols, chunk_cols), chunk_cols)
        pltpu.make_async_copy(queries_hbm.at[:, cols], q_own.at[g], load_sem.at[0]).start()
        pltpu.make_async_copy(keys_hbm.at[:, cols], kv_own.at[g, 0], load_sem.at[1]).start()
        pltpu.make_async_copy(values_hbm.at[:, cols], kv_own.at[g, 1], load_sem.at[1]).start()
        return carry

    queue_load = pltpu.make_async_copy(queue_hbm, queue.at[batch], load_sem.at[2])
    queue_load.start()
    lax.fori_loop(0, chunks, start_loads, 0)
    small_loads = [
        pltpu.make_async_copy(source, target, load_sem.at[5 + n])
        for n, (source, target) in enumerate(
            [(gain_hbm, gain_ref), (lengths_hbm, lengths_ref), (wanted_hbm, wanted_ref)]
        )
    ]
    for copy in small_loads:
        copy.start()
    residual_load = pltpu.make_async_copy(residual_hbm, residual, load_sem.at[3])
    weight_load = pltpu.make_async_copy(weight_hbm, weight, load_sem.at[4])

    for at in range(n_seq):

        @pl.when(seq == at)
        def _():
            pl.semaphore_wait(barrier, at + (at < n_seq - 1) + len(queue_peers))

    def tell_left():
        pl.semaphore_signal(
            higher_sem, inc=1, device_id={"seq": seq_peers[-1]}, device_id_type=MESH
        )

    @pl.when(seq == n_seq - 2)
    def _():
        tell_left()

    def hear_of_higher():
        pl.semaphore_wait(higher_sem, 1)

        @pl.when(seq >= 1)
        def _():
            tell_left()

    is_first = seq == 0
    is_second = seq == 1
    later = seq >= 2
    has_near = seq <= n_seq - 2

    left, left_two = lax.rem(seq + n_seq - 1, n_seq), lax.rem(seq + n_seq - 2, n_seq)
    right, right_two = lax.rem(seq + 1, n_seq), lax.rem(seq + 2, n_seq)

    def remote(kind, source, target, recv_sem, peer):
        return pltpu.make_async_remote_copy(
            src_ref=source,
            dst_ref=target,
            send_sem=send_sem.at[kind],
            recv_sem=recv_sem,
            device_id={"seq": peer},
            device_id_type=MESH,
        )

    def ask_near(g):
        return remote(0, q_own.at[g], q_near.at[g], asked_sem.at[0, g], left)

    def ask_far(g):
        return remote(1, q_own.at[g], q_far.at[g], asked_sem.at[1, g], left_two)

    def give_first(g):
        return remote(2, kv_own.at[g], kv_first.at[g], asked_sem.at[2, g], right)

    def give_near(at, t):
        return remote(3, near_out.at[at], near_in.at[at], given_sem.at[0, t], right)

    def give_near_log(t):
        return remote(4, near_out_log.at[t], near_in_log.at[t], given_sem.at[1, t], right)

    def give_far(at, t):
        return remote(5, far_out.at[at], far_in.at[at], given_sem.at[2, t], right_two)

    def give_far_log(t):
        return remote(6, far_out_log.at[t], far_in_log.at[t], given_sem.at[3, t], right_two)

    def queue_copy(shard, k, sem, p):
        return pltpu.make_async_remote_copy(
            src_ref=queue.at[shard, k],
            dst_ref=queue.at[shard, k],
            send_sem=queue_send.at[0],
            recv_sem=sem,
            device_id={"batch": queue_peers[p]},
            device_id_type=MESH,
        )

    def spread_own(k, carry):
        queue_copy(batch, k, queue_recv.at[0, k], 1).start()
        for d in range(1, n_col):
            queue_copy(batch, k, queue_recv.at[n_col - d, k], 1 + d).start()
        queue_copy(batch, k, beside_recv.at[0], 0).start()
        return carry

    def forward(k):
        for e, shard in enumerate([across] + along):
            queue_copy(shard, k, queue_recv.at[e, k], 1).wait_recv()

        @pl.when(lax.rem(k, 2) == 0)
        def _():
            for d in range(1, n_col):
                sem = queue_recv.at[n_col - 1 + n_col - d, k]
                queue_copy(across, k, sem, 1 + d).start()

        @pl.when(lax.rem(k, 2) == 1)
        def _():
            for e in range(1, n_col):
                queue_copy(along[e - 1], k, queue_recv.at[n_col - 1 + e, k], 1).start()

        for shard in [across] + along:
            queue_copy(shard, k, beside_recv.at[0], 0).start()

    def forward_diagonal(k):
        for e, shard in enumerate(diagonal):
            queue_copy(shard, k, queue_recv.at[n_col + e, k], 1).wait_recv()
            queue_copy(shard, k, beside_recv.at[1], 0).start()

    queue_load.wait()
    lax.fori_loop(0, pieces, spread_own, 0)
    pltpu.make_async_copy(q_own, q_own, load_sem.at[0]).wait()

    @pl.when(seq >= 3)
    def _():
        def ask_both(g, carry):
            @pl.when((seq > 3) | (g >= early))
            def _():
                ask_far(g).start()

            ask_near(g).start()
            return carry

        lax.fori_loop(0, chunks, ask_both, 0)

    @pl.when(seq == 2)
    def _():
        def ask_one(g, carry):
            ask_near(g).start()
            return carry

        lax.fori_loop(0, chunks, ask_one, 0)

    pltpu.make_async_copy(kv_own, kv_own, load_sem.at[1]).wait()

    @pl.when(is_first)
    def _():
        def give(g, carry):
            give_first(g).start()
            return carry

        lax.fori_loop(0, chunks, give, 0)

    @pl.when(is_second)
    def _():
        for g in range(early):
            give_first(g).start()


    residual_load.start()
    weight_load.start()
    for copy in small_loads:
        copy.wait()
    row_ids = lax.broadcasted_iota(jnp.int32, (funcs, funcs), 0)
    func_ids = lax.broadcasted_iota(jnp.int32, (funcs, funcs), 1)
    listed = lax.rem(row_ids, own_rows) * n_seq + row_ids // own_rows
    lengths = jnp.broadcast_to(lengths_ref[...].astype(F32), (funcs, funcs))
    begin_at = jnp.sum(jnp.where(func_ids < listed, lengths, 0.0), axis=1, keepdims=True)
    end_at = jnp.sum(jnp.where(func_ids <= listed, lengths, 0.0), axis=1, keepdims=True)
    pos = (
        seq * tok_rows + lax.broadcasted_iota(jnp.int32, (funcs, tok_rows), 1)
    ).astype(F32)
    member[...] = jnp.where((pos >= begin_at) & (pos < end_at), 1.0, 0.0).astype(BF16)

    def near_to(g, blocks):
        t, n = g // pair, lax.rem(g, pair)
        mixed, logs = attend(q_near[g], blocks, head_size)
        near_out_log[t, n] = logs
        near_out[g] = mixed.astype(BF16)
        give_near(g, t).start()

        @pl.when(n == pair - 1)
        def _():
            give_near_log(t).start()

    def far_to(g):
        t, n = g // pair, lax.rem(g, pair)
        ask_far(g).wait_recv()
        mixed, logs = attend(q_far[g], [own_keys(g) + (2,)], head_size)
        far_out_log[t, n] = logs
        far_out[g] = mixed.astype(BF16)
        give_far(g, t).start()

        @pl.when(n == pair - 1)
        def _():
            give_far_log(t).start()

    def own_keys(g):
        return (kv_own.at[g, 0], v_t.at[g])

    def first_keys(g):
        return (kv_first.at[g, 0], v_t_first.at[g])

    def await_first(g):
        give_first(g).wait_recv()
        v_t_first[g] = kv_first[g, 1].T

    if n_seq > 4:

        @pl.when((seq >= 2) & (seq <= n_seq - 3))
        def _():
            hear_of_higher()

    def step(g, carry):
        v_t[g] = kv_own[g, 1].T

        @pl.when(is_first)
        def _():
            mixed, _ = attend(q_own[g], [own_keys(g) + (0,)], head_size)
            att_t[g] = mixed.astype(BF16)

        @pl.when(is_second & (g < early))
        def _():
            await_first(g)
            ask_near(g).wait_recv()
            near_to(g, [first_keys(g) + (2,)])

        @pl.when(is_second & (g >= early))
        def _():
            far_to(g)
            await_first(g)
            ask_near(g).wait_recv()
            near_to(g, [own_keys(g) + (1,), first_keys(g) + (2,)])

        @pl.when(is_second)
        def _():
            mixed, _ = attend(q_own[g], [own_keys(g) + (0,), first_keys(g) + (1,)], head_size)
            att_t[g] = mixed.astype(BF16)

        third = (seq == 2) & (g < early)

        @pl.when(third)
        def _():
            await_first(g)
            ask_near(g).wait_recv()
            near_to(g, [own_keys(g) + (1,), first_keys(g) + (2,)])
            mixed, logs = attend(q_own[g], [own_keys(g) + (0,), first_keys(g) + (1,)], head_size)
            mix_own[g] = mixed
            log_own[g] = logs

        @pl.when(later & has_near & jnp.logical_not(third))
        def _():
            ask_near(g).wait_recv()
            near_to(g, [own_keys(g) + (1,)])

        if n_seq > 4:

            @pl.when(later & (seq <= n_seq - 3))
            def _():
                far_to(g)

        @pl.when(later & jnp.logical_not(third))
        def _():
            mixed, logs = attend(q_own[g], [own_keys(g) + (0,)], head_size)
            mix_own[g] = mixed
            log_own[g] = logs

        @pl.when((g == early - 1) & (seq <= 1))
        def _():
            hear_of_higher()

        @pl.when((g >= 2) & (g <= 2 * pieces) & (lax.rem(g, 2) == 0))
        def _():
            forward(g // 2 - 1)

        return carry

    lax.fori_loop(0, chunks, step, 0)
    for k in range(min(chunks // 2 - 1, pieces), pieces):
        forward(k)

    residual_load.wait()
    weight_load.wait()
    hidden[...] = residual[...].astype(F32)

    def project(t, carry):
        both = pl.ds(t * pair, pair)

        @pl.when(later)
        def _():
            give_near(both, t).wait_recv()
            give_near_log(t).wait_recv()

        @pl.when((seq == 2) | ((seq == 3) & (t == 0)))
        def _():
            for n in range(pair):
                g = t * pair + n
                att_t[g] = merge(
                    [(mix_own[g], log_own[g]), (near_in[g], near_in_log[t, n])], heads, head_size
                )

        @pl.when((seq > 3) | ((seq == 3) & (t > 0)))
        def _():
            give_far(both, t).wait_recv()
            give_far_log(t).wait_recv()
            for n in range(pair):
                g = t * pair + n
                att_t[g] = merge(
                    [
                        (mix_own[g], log_own[g]),
                        (near_in[g], near_in_log[t, n]),
                        (far_in[g], far_in_log[t, n]),
                    ],
                    heads,
                    head_size,
                )

        depth = pair * chunk_cols
        hidden[...] += lax.dot_general(
            att_t[both].reshape(depth, tok_rows),
            weight[pl.ds(pl.multiple_of(t * depth, depth), depth), :],
            (((0,), (0,)), ((), ())),
            preferred_element_type=F32,
        )
        return carry

    lax.fori_loop(0, chunks // pair, project, 0)

    total = hidden[...]
    scale = lax.rsqrt(jnp.mean(total * total, axis=-1, keepdims=True) + 1e-05)
    normed = (total * scale * gain_ref[...]).astype(BF16)
    partial = jnp.dot(member[...], normed, preferred_element_type=F32)
    parts[...] = partial.reshape(n_seq, own_rows, width).astype(BF16)
    def part_copy(source, target, peer):
        return pltpu.make_async_remote_copy(
            src_ref=source,
            dst_ref=target,
            send_sem=part_sem.at[0],
            recv_sem=part_sem.at[1],
            device_id={"seq": peer},
            device_id_type=MESH,
        )

    for d in range(1, n_seq):
        peer = seq_peers[d - 1]
        part_copy(parts.at[peer], parts_in.at[d - 1], peer).start()
    for k in range(pieces // 2):
        forward_diagonal(k)
    all_parts = part_copy(parts_in, parts_in, right)
    all_parts.wait_recv()
    pooled = parts[seq].astype(F32)
    for d in range(1, n_seq):
        pooled = pooled + parts_in[d - 1].astype(F32)
    anchors = (
        pooled * lax.rsqrt(jnp.sum(pooled * pooled, axis=-1, keepdims=True) + 1e-06)
    ).astype(BF16)
    anchors_ref[...] = anchors

    def logits_of(shard):
        logits[shard] = LOGIT_SCALE * lax.dot_general(
            anchors,
            queue[shard].reshape(queue_rows, width),
            ROWS_T,
            preferred_element_type=F32,
        )

    def await_beside(at, shards):
        ref = queue.at[pl.ds(0, shards)]
        pltpu.make_async_remote_copy(
            src_ref=ref,
            dst_ref=ref,
            send_sem=queue_send.at[0],
            recv_sem=beside_recv.at[at],
            device_id={"batch": sibling},
            device_id_type=MESH,
        ).wait_recv()

    for shard in [batch, across] + along:
        logits_of(shard)
    for k in range(pieces // 2, pieces):
        forward_diagonal(k)
    await_beside(0, n_col + 1)
    for shard in [sibling, shard_at(col, 1 - row, 1 - core)]:
        logits_of(shard)
    for c in cols_away:
        logits_of(shard_at(c, row, 1 - core))
    for shard in diagonal:
        logits_of(shard)
    await_beside(1, n_col - 1)
    for c in cols_away:
        logits_of(shard_at(c, 1 - row, 1 - core))

    square = (own_rows, own_rows)
    on_diagonal = lax.broadcasted_iota(jnp.int32, square, 0) == lax.broadcasted_iota(
        jnp.int32, square, 1
    )
    wanted = jnp.broadcast_to(wanted_ref[pl.ds(batch, 1), :].astype(F32), square)
    wanted = jnp.sum(jnp.where(on_diagonal, wanted, 0.0), axis=1, keepdims=True)
    wanted = wanted.astype(jnp.int32)
    peak = functools.reduce(
        jnp.maximum, [jnp.max(logits[b], axis=1, keepdims=True) for b in range(n_batch)]
    )
    lane = lax.broadcasted_iota(jnp.int32, (own_rows, queue_rows), 1)
    sums, chosen = 0.0, 0.0
    for b in range(n_batch):
        sums = sums + jnp.exp(logits[b] - peak)
        chosen = chosen + jnp.where(lane + b * queue_rows == wanted, logits[b], 0.0)
    loss = (
        peak
        + jnp.log(jnp.sum(sums, axis=1, keepdims=True))
        - jnp.sum(chosen, axis=1, keepdims=True)
    )
    losses_ref[...] = jnp.sum(
        jnp.where(on_diagonal, jnp.broadcast_to(loss, square), 0.0), axis=0, keepdims=True
    )

    all_parts.wait_send()
    sent = queue.at[pl.ds(0, n_batch - 1)]
    pltpu.make_async_remote_copy(
        src_ref=sent,
        dst_ref=sent,
        send_sem=queue_send.at[0],
        recv_sem=beside_recv.at[0],
        device_id={"batch": sibling},
        device_id_type=MESH,
    ).wait_send()

    def sent_all(kind, ref):
        remote(kind, ref, ref, given_sem.at[0, 0], right).wait_send()

    @pl.when(is_first)
    def _():
        sent_all(2, kv_own)

    @pl.when(later)
    def _():
        sent_all(0, q_own)

    late = pl.ds(early, chunks - early)

    @pl.when(is_second)
    def _():
        sent_all(2, kv_own.at[pl.ds(0, early)])

    @pl.when(seq == 3)
    def _():
        sent_all(1, q_own.at[late])

    @pl.when(seq > 3)
    def _():
        sent_all(1, q_own)

    @pl.when((seq >= 1) & has_near)
    def _():
        sent_all(3, near_out)
        sent_all(4, near_out_log)

    @pl.when(is_second)
    def _():
        sent_all(5, far_out.at[late])
        sent_all(6, far_out_log.at[pl.ds(1, chunks // pair - 1)])

    if n_seq > 4:

        @pl.when(later & (seq <= n_seq - 3))
        def _():
            sent_all(5, far_out)
            sent_all(6, far_out_log)


def body(
    queries, keys, values, residual, out_weight, norm_gain, source_queue, span_lengths, positives
):
    tok_rows, width = queries.shape[1:]
    head_size = width // HEADS
    n_seq = lax.axis_size("seq")
    n_batch = lax.axis_size("batch")
    own_rows = positives.shape[1]
    queue_rows = source_queue.shape[0]
    chunk_cols = 128
    chunks = width // chunk_cols
    pieces = max(2, 32 // n_batch)
    pair = 2
    piece_rows = queue_rows // pieces
    assert (WINDOW - 1) // tok_rows + 1 == 2 and chunk_cols % head_size == 0
    assert n_seq >= 4 and n_batch % 4 == 0 and pieces % 2 == 0 and piece_rows % 16 == 0
    vmem = pl.BlockSpec(memory_space=pltpu.VMEM)
    hbm = pl.BlockSpec(memory_space=pl.ANY)
    rows_bf16 = pltpu.VMEM((chunks, tok_rows, chunk_cols), BF16)
    cols_bf16 = pltpu.VMEM((chunks, chunk_cols, tok_rows), BF16)
    cols_f32 = pltpu.VMEM((chunks, chunk_cols, tok_rows), F32)
    log_f32 = pltpu.VMEM((chunks // pair, pair, chunk_cols // head_size, tok_rows), F32)
    kv_bf16 = pltpu.VMEM((chunks, 2, tok_rows, chunk_cols), BF16)
    anchors, losses = pl.pallas_call(
        functools.partial(block_kernel, n_seq, n_batch, head_size),
        out_shape=(
            jax.ShapeDtypeStruct((own_rows, width), BF16),
            jax.ShapeDtypeStruct((1, own_rows), F32),
        ),
        in_specs=[hbm] * 9,
        out_specs=(vmem, vmem),
        scratch_shapes=[
            rows_bf16,
            kv_bf16,
            cols_bf16,
            rows_bf16,
            rows_bf16,
            kv_bf16,
            cols_bf16,
            cols_f32,
            pltpu.VMEM((chunks, chunk_cols // head_size, tok_rows), F32),
            cols_bf16,
            log_f32,
            cols_bf16,
            log_f32,
            cols_bf16,
            log_f32,
            cols_bf16,
            log_f32,
            cols_bf16,
            pltpu.VMEM((tok_rows, width), BF16),
            pltpu.VMEM(out_weight.shape, BF16),
            pltpu.VMEM((tok_rows, width), F32),
            pltpu.VMEM((own_rows * n_seq, tok_rows), BF16),
            pltpu.VMEM((n_batch, pieces, piece_rows, width), BF16),
            pltpu.VMEM((n_seq, own_rows, width), BF16),
            pltpu.VMEM((n_seq - 1, own_rows, width), BF16),
            pltpu.VMEM((n_batch, own_rows, queue_rows), F32),
            pltpu.SemaphoreType.DMA((8,)),
            pltpu.SemaphoreType.DMA((7,)),
            pltpu.SemaphoreType.DMA((3, chunks)),
            pltpu.SemaphoreType.DMA((4, chunks // pair)),
            pltpu.SemaphoreType.DMA((2,)),
            pltpu.SemaphoreType.DMA((1,)),
            pltpu.SemaphoreType.DMA((n_batch // 2 - 1, pieces)),
            pltpu.SemaphoreType.DMA((2,)),
            pltpu.SemaphoreType.REGULAR,
            pltpu.VMEM((1, width), F32),
            pltpu.VMEM(span_lengths.shape, jnp.int32),
            pltpu.VMEM(positives.shape, jnp.int32),
        ],
        compiler_params=pltpu.CompilerParams(
            collective_id=0, has_side_effects=True, vmem_limit_bytes=67043328
        ),
        name="block",
    )(
        norm_gain.reshape(1, -1),
        span_lengths,
        positives,
        queries[0],
        keys[0],
        values[0],
        residual[0],
        out_weight,
        source_queue.reshape(pieces, piece_rows, width),
    )

    def hand_on(anchors_ref, losses_ref, anchors_out, losses_out):
        anchors_out[...] = anchors_ref[...]
        losses_out[...] = losses_ref[...]

    anchors, losses = pl.pallas_call(
        hand_on,
        out_shape=(
            jax.ShapeDtypeStruct((own_rows, width), BF16),
            jax.ShapeDtypeStruct((1, own_rows), F32),
        ),
        in_specs=[vmem] * 2,
        out_specs=(vmem, vmem),
        name="hand_on",
    )(anchors, losses)
    return (anchors[None], losses)


def solution(mesh):
    return jax.shard_map(
        body,
        mesh=mesh,
        in_specs=(
            P("batch", "seq", None),
            P("batch", "seq", None),
            P("batch", "seq", None),
            P("batch", "seq", None),
            P(),
            P(),
            P("batch", None),
            P("batch", None),
            P(None, "seq"),
        ),
        out_specs=(P("batch", "seq", None), P("batch", "seq")),
        check_vma=False,
    )
```
